128 devices in a mesh: section: 4 (over y), seq: 32 (over z, x, core).
Axes of the slice: x: 4, y: 4, z: 4, core: 2. Of those that a mesh axis runs over, the one named last changes fastest.
Arguments:
- layer_input: bfloat16 [4, 2, 2048, 8192], P('section', None, 'seq'), may hold values from -60 to 60
- query_act: bfloat16 [4, 2, 2048, 8192], P('section', None, 'seq'), may hold values from -8 to 8
- key_act: bfloat16 [4, 2, 2048, 1024], P('section', None, 'seq'), may hold values from -6 to 6
- value_act: bfloat16 [4, 2, 2048, 1024], P('section', None, 'seq'), may hold values from -6 to 6
- output_grad: bfloat16 [4, 2, 2048, 8192], P('section', None, 'seq'), may hold values from -24 to 24
- value_weight: bfloat16 [4, 8192, 1024], P('section', 'seq'), may hold values from -0.0625 to 0.0625
- norm_gain: float32 [4, 8192], P('section'), may hold values from 0.1 to 1.9
- top_grad: bfloat16 [2, 2048, 8192], P(None, 'seq'), may hold values from -3 to 3
Outputs:
- input_grad: bfloat16 [4, 2, 2048, 8192], P('section', None, 'seq')
- query_grad: bfloat16 [4, 2, 2048, 8192], P('section', None, 'seq')
- key_grad: bfloat16 [4, 2, 2048, 1024], P('section', None, 'seq')
The draws below stay inside these ranges and needn't reach their ends.
All inputs are finite; a program needn't handle non-finite values.
Results may differ from the reference program's by a relative error of at most 0.015.
Values may be sent and summed in bfloat16 or wider, within the bound.
No kernel may reach another device: no remote copies, remote signals or barrier semaphores. Data moves between devices by JAX's collectives and lax.ppermute only.
A program may use at most 192 MiB of HBM per device.

```python
import math
import jax
import jax.numpy as jnp
from jax import lax

D = 8192
HEADS = 64
KV_HEADS = 8
HEAD_DIM = 128
BATCH = 2
SEQ_LEN = 2048
SECTIONS = 4


def draw_query_act(key, part):
    base_key = jax.random.fold_in(key, 3)
    shape_full = (SECTIONS, BATCH, SEQ_LEN, KV_HEADS, HEADS // KV_HEADS, HEAD_DIM)
    values_drawn = jnp.clip(jax.random.normal(base_key, shape_full, jnp.float32), -6.0, 6.0)
    return values_drawn.reshape(SECTIONS, BATCH, SEQ_LEN, HEADS * HEAD_DIM).astype(jnp.bfloat16)


def draw_key_act(key, part):
    base_key = jax.random.fold_in(key, 5)
    shape_full = (SECTIONS, BATCH, SEQ_LEN, KV_HEADS, HEAD_DIM)
    values_drawn = jnp.clip(jax.random.normal(base_key, shape_full, jnp.float32), -6.0, 6.0)
    return values_drawn.reshape(SECTIONS, BATCH, SEQ_LEN, KV_HEADS * HEAD_DIM).astype(jnp.bfloat16)


def draw_layer_input(key, part):
    subkeys = jax.random.split(jax.random.fold_in(key, 21), 3)
    shape_full = (SECTIONS, BATCH, SEQ_LEN, D)
    values_drawn = jnp.clip(jax.random.normal(subkeys[0], shape_full, jnp.float32), -4.0, 4.0)
    row_scale = jnp.exp(jax.random.uniform(subkeys[1], (SECTIONS, BATCH, SEQ_LEN, 1), jnp.float32, math.log(0.3), math.log(3.0)))
    column_scale = jnp.exp(jax.random.uniform(subkeys[2], (SECTIONS, 1, 1, D), jnp.float32, math.log(0.5), math.log(5.0)))
    return (values_drawn * row_scale * column_scale).astype(jnp.bfloat16)


def block_levels(stream_key, shape, shards, low, high):
    level, own = 1.0, jax.random.fold_in(stream_key, 6)
    for axis_at, blocks in shards:
        draws = jnp.exp(jax.random.uniform(jax.random.fold_in(own, axis_at), (blocks,), jnp.float32, low / len(shards), high / len(shards)))
        level = level * jnp.repeat(draws, shape[axis_at] // blocks).reshape([-1 if axis == axis_at else 1 for axis in range(len(shape))])
    return level


def centred(rng, extent, width, reach, cuts=(), held_as=jnp.bfloat16):
    loudness = block_levels(rng, extent, cuts, -0.22, 0.18) if cuts else 1.0
    drawn = jax.random.normal(rng, extent, jnp.float32) * width * loudness
    return jnp.minimum(jnp.maximum(drawn, -reach), reach).astype(held_as)


def setup_inputs(seed: int = 0) -> dict:
    arg_keys = jax.random.split(jax.random.key(seed), 9)
    layer_input = draw_layer_input(jax.random.fold_in(arg_keys[8], 71), 0)
    query_act = draw_query_act(jax.random.fold_in(arg_keys[8], 71), 0)
    key_act = draw_key_act(jax.random.fold_in(arg_keys[8], 71), 0)
    value_act = centred(arg_keys[3], (SECTIONS, BATCH, SEQ_LEN, KV_HEADS * HEAD_DIM), 1.0, 6.0, ((0, 4), (2, 32)))
    output_grad = jnp.clip(jax.random.uniform(arg_keys[4], (SECTIONS, BATCH, SEQ_LEN, D), jnp.float32, -24.0, 24.0) * block_levels(arg_keys[4], (SECTIONS, BATCH, SEQ_LEN, D), ((0, 4), (2, 32)), -0.4, 0.0), -24.0, 24.0).astype(jnp.bfloat16)
    value_weight = centred(arg_keys[5], (SECTIONS, D, KV_HEADS * HEAD_DIM), D ** -0.5, 0.0625, ((0, 4), (1, 32)))
    norm_gain = jnp.clip(1.0 + 0.18 * jax.random.normal(arg_keys[6], (SECTIONS, D), jnp.float32), 0.1, 1.9)
    top_grad = centred(arg_keys[7], (BATCH, SEQ_LEN, D), 0.5, 3.0, ((1, 32),))
    return dict(layer_input=layer_input, query_act=query_act, key_act=key_act, value_act=value_act, output_grad=output_grad, value_weight=value_weight, norm_gain=norm_gain, top_grad=top_grad)


def group_grads(query_rows, grad_rows, key_rows, value_rows):
    length = key_rows.shape[0]
    block_rows = min(512, length)
    score_scale = key_rows.shape[1] ** (-0.5)
    key_pos = jnp.arange(length, dtype=jnp.int32)
    key_full = key_rows.astype(jnp.float32)
    value_full = value_rows.astype(jnp.float32)

    def step(totals, block_index):
        key_total, value_total = totals
        block_start = (block_index * block_rows).astype(jnp.int32)
        query_block = lax.dynamic_slice_in_dim(query_rows, block_start, block_rows, 0).astype(jnp.float32)
        grad_block = lax.dynamic_slice_in_dim(grad_rows, block_start, block_rows, 0).astype(jnp.float32)
        scores = jnp.einsum('qgd,kd->gqk', query_block, key_full) * score_scale
        query_pos = block_start + jnp.arange(block_rows, dtype=jnp.int32)
        visible = key_pos[None, :] <= query_pos[:, None]
        scores = jnp.where(visible[None], scores, jnp.float32(-1e+30))
        row_top = lax.optimization_barrier(jnp.max(scores, axis=-1, keepdims=True))
        raised = jnp.exp(scores - row_top)
        weights = raised / lax.optimization_barrier(jnp.sum(raised, axis=-1, keepdims=True))
        weights_low = lax.optimization_barrier(weights.astype(jnp.bfloat16)).astype(jnp.float32)
        value_total = value_total + jnp.einsum('gqk,qgd->kd', weights_low, grad_block)
        prob_grad = jnp.einsum('qgd,kd->gqk', grad_block, value_full)
        center = lax.optimization_barrier(jnp.sum(weights * prob_grad, axis=-1, keepdims=True))
        score_grad = lax.optimization_barrier((weights * (prob_grad - center)).astype(jnp.bfloat16)).astype(jnp.float32)
        query_out = (jnp.einsum('gqk,kd->qgd', score_grad, key_full) * score_scale).astype(jnp.bfloat16)
        key_total = key_total + jnp.einsum('gqk,qgd->kd', score_grad, query_block) * score_scale
        return ((key_total, value_total), query_out)
    empty = jnp.zeros((length, key_rows.shape[1]), jnp.float32)
    (key_total, value_total), query_out = lax.scan(step, (empty, empty), jnp.arange(length // block_rows, dtype=jnp.int32))
    return (query_out.reshape(length, query_rows.shape[1], query_rows.shape[2]), key_total, value_total)

def norm_back(rows, gain, upstream):
    rows_full = rows.astype(jnp.float32)
    inverse_rms = lax.rsqrt(lax.optimization_barrier(jnp.mean(rows_full * rows_full, axis=-1, keepdims=True)) + 1e-05)
    scaled = gain.astype(jnp.float32)[None, :] * upstream
    inner = lax.optimization_barrier(jnp.mean(scaled * rows_full, axis=-1, keepdims=True))
    return inverse_rms * scaled - rows_full * (inverse_rms * inverse_rms * inverse_rms) * inner

def reference(layer_input, query_act, key_act, value_act, output_grad, value_weight, norm_gain, top_grad):
    group_size = HEADS // KV_HEADS
    kv_width = KV_HEADS * HEAD_DIM

    def one_group(operands):
        return group_grads(operands[0], operands[1], operands[2], operands[3])
    section_terms = []
    query_list = []
    key_list = []
    for section_index in range(SECTIONS):
        term_rows = []
        query_rows_list = []
        key_rows_list = []
        for seq_index in range(BATCH):
            query_rows = query_act[section_index, seq_index].reshape(SEQ_LEN, KV_HEADS, group_size, HEAD_DIM).transpose(1, 0, 2, 3)
            grad_rows = output_grad[section_index, seq_index].reshape(SEQ_LEN, KV_HEADS, group_size, HEAD_DIM).transpose(1, 0, 2, 3)
            key_rows = key_act[section_index, seq_index].reshape(SEQ_LEN, KV_HEADS, HEAD_DIM).transpose(1, 0, 2)
            value_rows = value_act[section_index, seq_index].reshape(SEQ_LEN, KV_HEADS, HEAD_DIM).transpose(1, 0, 2)
            query_out, key_total, value_total = lax.map(one_group, (query_rows, grad_rows, key_rows, value_rows))
            query_rows_list.append(query_out.transpose(1, 0, 2, 3).reshape(SEQ_LEN, HEADS * HEAD_DIM))
            key_rows_list.append(key_total.transpose(1, 0, 2).reshape(SEQ_LEN, kv_width).astype(jnp.bfloat16))
            value_low = value_total.transpose(1, 0, 2).reshape(SEQ_LEN, kv_width).astype(jnp.bfloat16)
            norm_grad = jnp.dot(value_low, value_weight[section_index].T, preferred_element_type=jnp.float32)
            term_rows.append(norm_back(layer_input[section_index, seq_index], norm_gain[section_index], norm_grad))
        section_terms.append(jnp.stack(term_rows))
        query_list.append(jnp.stack(query_rows_list))
        key_list.append(jnp.stack(key_rows_list))
    input_list = [None] * SECTIONS
    current = (top_grad.astype(jnp.float32) + section_terms[SECTIONS - 1]).astype(jnp.bfloat16)
    input_list[SECTIONS - 1] = current
    for section_index in range(SECTIONS - 2, -1, -1):
        current = (current.astype(jnp.float32) + section_terms[section_index]).astype(jnp.bfloat16)
        input_list[section_index] = current
    return (jnp.stack(input_list), jnp.stack(query_list), jnp.stack(key_list))
```

```python
import functools

import jax
import jax.numpy as jnp
from jax import lax
from jax.experimental import pallas as pl
from jax.experimental.pallas import tpu as pltpu
from jax.sharding import PartitionSpec as P

D = 8192
KV_HEADS = 8
HEAD_DIM = 128
BATCH = 2
SEQ = 2048
DEVICES = 32
LOCAL = SEQ // DEVICES
UNIT_HEADS = 4
QCOLS = UNIT_HEADS * HEAD_DIM
UNITS = DEVICES // BATCH
PACK = 2 * QCOLS + 2 * HEAD_DIM
TOK = 128
BLOCKS = SEQ // TOK
CHUNK = 256
CHUNKS = SEQ // CHUNK
SCALE = HEAD_DIM ** (-0.5)
LOG2E = 1.4426950408889634
NEG = -1e30

BF = jnp.bfloat16
F32 = jnp.float32
LAST = (((1,), (1,)), ((), ()))


def pack_body(q_ref, g_ref, k_ref, v_ref, out_ref, sem):
    copies = []
    for dest in range(DEVICES):
        seq, unit = dest // UNITS, dest % UNITS
        head = unit // 2
        for src, width, start, at in (
            (q_ref, QCOLS, unit * QCOLS, 0),
            (g_ref, QCOLS, unit * QCOLS, QCOLS),
            (k_ref, HEAD_DIM, head * HEAD_DIM, 2 * QCOLS),
            (v_ref, HEAD_DIM, head * HEAD_DIM, 2 * QCOLS + HEAD_DIM),
        ):
            copies.append(
                pltpu.make_async_copy(
                    src.at[seq, :, pl.ds(start, width)],
                    out_ref.at[dest, :, pl.ds(at, width)],
                    sem.at[len(copies)],
                )
            )
    for copy in copies:
        copy.start()
    for copy in copies:
        copy.wait()


def pack(q, g, k, v):
    return pl.pallas_call(
        pack_body,
        out_shape=jax.ShapeDtypeStruct((DEVICES, LOCAL, PACK), BF),
        in_specs=[pl.BlockSpec(memory_space=pl.ANY)] * 4,
        out_specs=pl.BlockSpec(memory_space=pl.ANY),
        scratch_shapes=[pltpu.SemaphoreType.DMA((4 * DEVICES,))],
        name="pack",
    )(q, g, k, v)


def unpack_body(in_ref, out_ref, sem):
    copies = []
    for source in range(DEVICES):
        seq, unit = source // UNITS, source % UNITS
        copies.append(
            pltpu.make_async_copy(
                in_ref.at[source],
                out_ref.at[seq, :, pl.ds(unit * QCOLS, QCOLS)],
                sem.at[source],
            )
        )
    for copy in copies:
        copy.start()
    for copy in copies:
        copy.wait()


def unpack(parts):
    return pl.pallas_call(
        unpack_body,
        out_shape=jax.ShapeDtypeStruct((BATCH, LOCAL, D), BF),
        in_specs=[pl.BlockSpec(memory_space=pl.ANY)],
        out_specs=pl.BlockSpec(memory_space=pl.ANY),
        scratch_shapes=[pltpu.SemaphoreType.DMA((DEVICES,))],
        name="unpack",
    )(parts)


def stack_heads(ref):
    return jnp.concatenate(
        [ref[:, h * HEAD_DIM : (h + 1) * HEAD_DIM] for h in range(UNIT_HEADS)], axis=0
    )


def fold(chunk, op):
    return op(chunk.reshape(CHUNK // 8, 8, QCOLS), axis=0)


def probs_body(q_ref, g_ref, k_ref, e_ref, l_ref, dv_ref, s_ref, dv_acc):
    block = pl.program_id(0)
    last = block // 2

    @pl.when(block == 0)
    def _():
        dv_acc[...] = jnp.zeros_like(dv_acc)

    q = stack_heads(q_ref)

    def score(c):
        rows = pl.ds(pl.multiple_of(c * CHUNK, CHUNK), CHUNK)
        return lax.dot_general(k_ref[rows, :], q, LAST, preferred_element_type=F32)

    def sweep_score(c, top):
        s = score(c)
        s_ref[c] = s
        return jnp.maximum(top, fold(s, jnp.max))

    top = lax.fori_loop(0, last, sweep_score, jnp.full((8, QCOLS), NEG, F32))
    s = score(last)
    key_pos = last * CHUNK + lax.broadcasted_iota(jnp.int32, (CHUNK, QCOLS), 0)
    query_pos = block * TOK + lax.broadcasted_iota(jnp.int32, (CHUNK, QCOLS), 1) % TOK
    s = jnp.where(key_pos <= query_pos, s, NEG)
    s_ref[last] = s
    top = jnp.max(jnp.maximum(top, fold(s, jnp.max)), axis=0, keepdims=True)
    factor = SCALE * LOG2E

    def sweep_exp(c, total):
        e = jnp.exp2((s_ref[c] - top) * factor)
        e_ref[c] = e.astype(BF)
        return total + fold(e, jnp.sum)

    total = lax.fori_loop(0, last + 1, sweep_exp, jnp.zeros((8, QCOLS), F32))
    total = jnp.sum(total, axis=0, keepdims=True)
    inverse = 1.0 / total
    l_ref[...] = inverse
    column = jnp.transpose(jnp.broadcast_to(inverse, (HEAD_DIM, QCOLS)))
    g = (stack_heads(g_ref).astype(F32) * column).astype(BF)

    def sweep_dv(c, carry):
        rows = pl.ds(pl.multiple_of(c * CHUNK, CHUNK), CHUNK)
        dv_acc[rows, :] += jnp.dot(e_ref[c], g, preferred_element_type=F32)
        return carry

    lax.fori_loop(0, last + 1, sweep_dv, 0)

    @pl.when(block == BLOCKS - 1)
    def _():
        dv_ref[...] = dv_acc[...].astype(BF)


def attend_probs(packed):
    return pl.pallas_call(
        probs_body,
        grid=(BLOCKS,),
        out_shape=(
            jax.ShapeDtypeStruct((BLOCKS, CHUNKS, CHUNK, QCOLS), BF),
            jax.ShapeDtypeStruct((BLOCKS, 1, QCOLS), F32),
            jax.ShapeDtypeStruct((SEQ, HEAD_DIM), BF),
        ),
        in_specs=[
            pl.BlockSpec((TOK, QCOLS), lambda t: (t, 0)),
            pl.BlockSpec((TOK, QCOLS), lambda t: (t, 1)),
            pl.BlockSpec((SEQ, HEAD_DIM), lambda t: (0, 8)),
        ],
        out_specs=(
            pl.BlockSpec((None, CHUNKS, CHUNK, QCOLS), lambda t: (t, 0, 0, 0)),
            pl.BlockSpec((None, 1, QCOLS), lambda t: (t, 0, 0)),
            pl.BlockSpec((SEQ, HEAD_DIM), lambda t: (0, 0)),
        ),
        scratch_shapes=[
            pltpu.VMEM((CHUNKS, CHUNK, QCOLS), F32),
            pltpu.VMEM((SEQ, HEAD_DIM), F32),
        ],
        compiler_params=pltpu.CompilerParams(vmem_limit_bytes=40 << 20),
        name="probs",
    )(packed, packed, packed)


def grads_body(q_ref, g_ref, k_ref, v_ref, e_ref, l_ref, dq_ref, dk_ref, p_ref, kt_ref, dk_acc):
    block = pl.program_id(0)
    last = block // 2

    @pl.when(block == 0)
    def _():
        dk_acc[...] = jnp.zeros_like(dk_acc)
        for c in range(CHUNKS):
            kt_ref[c] = jnp.transpose(k_ref[c * CHUNK : (c + 1) * CHUNK, :])

    q = stack_heads(q_ref)
    inverse = l_ref[...]
    column = jnp.transpose(jnp.broadcast_to(inverse, (HEAD_DIM, QCOLS)))
    g = (stack_heads(g_ref).astype(F32) * column).astype(BF)

    def sweep_dp(c, total):
        rows = pl.ds(pl.multiple_of(c * CHUNK, CHUNK), CHUNK)
        p = lax.dot_general(v_ref[rows, :], g, LAST, preferred_element_type=F32)
        p_ref[c] = p
        return total + fold(p * e_ref[c].astype(F32), jnp.sum)

    total = lax.fori_loop(0, last + 1, sweep_dp, jnp.zeros((8, QCOLS), F32))
    center = jnp.sum(total, axis=0, keepdims=True) * inverse

    def sweep_ds(c, dq):
        rows = pl.ds(pl.multiple_of(c * CHUNK, CHUNK), CHUNK)
        ds = (e_ref[c].astype(F32) * (p_ref[c] - center)).astype(BF)
        dk_acc[rows, :] += jnp.dot(ds, q, preferred_element_type=F32)
        return dq + jnp.dot(kt_ref[c], ds, preferred_element_type=F32)

    dq = lax.fori_loop(0, last + 1, sweep_ds, jnp.zeros((HEAD_DIM, QCOLS), F32)) * SCALE
    for h in range(UNIT_HEADS):
        cols = slice(h * HEAD_DIM, (h + 1) * HEAD_DIM)
        dq_ref[:, cols] = jnp.transpose(dq[:, cols]).astype(BF)

    @pl.when(block == BLOCKS - 1)
    def _():
        dk_ref[...] = (dk_acc[...] * SCALE).astype(BF)


def attend_grads(packed, e, inverse):
    return pl.pallas_call(
        grads_body,
        grid=(BLOCKS,),
        out_shape=(
            jax.ShapeDtypeStruct((SEQ, QCOLS), BF),
            jax.ShapeDtypeStruct((SEQ, HEAD_DIM), BF),
        ),
        in_specs=[
            pl.BlockSpec((TOK, QCOLS), lambda t: (t, 0)),
            pl.BlockSpec((TOK, QCOLS), lambda t: (t, 1)),
            pl.BlockSpec((SEQ, HEAD_DIM), lambda t: (0, 8)),
            pl.BlockSpec((SEQ, HEAD_DIM), lambda t: (0, 9)),
            pl.BlockSpec((None, CHUNKS, CHUNK, QCOLS), lambda t: (t, 0, 0, 0)),
            pl.BlockSpec((None, 1, QCOLS), lambda t: (t, 0, 0)),
        ],
        out_specs=(
            pl.BlockSpec((TOK, QCOLS), lambda t: (t, 0)),
            pl.BlockSpec((SEQ, HEAD_DIM), lambda t: (0, 0)),
        ),
        scratch_shapes=[
            pltpu.VMEM((CHUNKS, CHUNK, QCOLS), F32),
            pltpu.VMEM((CHUNKS, HEAD_DIM, CHUNK), BF),
            pltpu.VMEM((SEQ, HEAD_DIM), F32),
        ],
        compiler_params=pltpu.CompilerParams(vmem_limit_bytes=40 << 20),
        name="grads",
    )(packed, packed, packed, packed, e, inverse)


ROWS = BATCH * LOCAL
FEATS = 1024


def term_body(vg_ref, w_ref, x_ref, gain_ref, top_ref, flag_ref, out_ref, u_ref, xs_ref, acc):
    step = pl.program_id(0)

    @pl.when(step == 0)
    def _():
        acc[...] = jnp.zeros_like(acc)

    u = lax.dot_general(vg_ref[...], w_ref[...], LAST, preferred_element_type=F32) * gain_ref[...]
    x = x_ref[...].astype(F32)
    u_ref[step] = u
    acc[0] += jnp.sum(x * x, axis=1, keepdims=True)
    acc[1] += jnp.sum(x * u, axis=1, keepdims=True)
    xs_ref[step] = x_ref[...]

    @pl.when(step == pl.num_programs(0) - 1)
    def _():
        r = lax.rsqrt(acc[0] * (1.0 / D) + 1e-05)
        inner = acc[1] * (1.0 / D) * (r * r * r)
        for i in range(D // FEATS):
            cols = slice(i * FEATS, (i + 1) * FEATS)
            term = r * u_ref[i] - xs_ref[i].astype(F32) * inner
            term = term + top_ref[:, cols].astype(F32) * flag_ref[0]
            out_ref[:, cols] = term.astype(BF)


def norm_term(vg, weight, x, gain, top, flag):
    steps = D // FEATS
    return pl.pallas_call(
        term_body,
        grid=(steps,),
        out_shape=jax.ShapeDtypeStruct((ROWS, D), BF),
        in_specs=[
            pl.BlockSpec((ROWS, KV_HEADS * HEAD_DIM), lambda i: (0, 0)),
            pl.BlockSpec((FEATS, KV_HEADS * HEAD_DIM), lambda i: (i, 0)),
            pl.BlockSpec((ROWS, FEATS), lambda i: (0, i)),
            pl.BlockSpec((1, FEATS), lambda i: (0, i)),
            pl.BlockSpec((ROWS, D), lambda i: (0, 0)),
            pl.BlockSpec(memory_space=pltpu.SMEM),
        ],
        out_specs=pl.BlockSpec((ROWS, D), lambda i: (0, 0)),
        scratch_shapes=[
            pltpu.VMEM((steps, ROWS, FEATS), F32),
            pltpu.VMEM((steps, ROWS, FEATS), BF),
            pltpu.VMEM((2, ROWS, 1), F32),
        ],
        compiler_params=pltpu.CompilerParams(vmem_limit_bytes=40 << 20),
        name="term",
    )(vg, weight, x, gain, top, flag)


def exchange(parts):
    return lax.all_to_all(parts, "seq", 0, 0, tiled=True)


def pair_sum(parts):
    both = parts.reshape(BATCH, KV_HEADS, 2, LOCAL, HEAD_DIM).astype(F32)
    total = (both[:, :, 0] + both[:, :, 1]).astype(BF)
    return jnp.concatenate([total[:, g] for g in range(KV_HEADS)], axis=-1)


def local(
    layer_input, query_act, key_act, value_act, output_grad, value_weight, norm_gain, top_grad
):
    weight = lax.all_gather(value_weight[0], "seq", axis=0, tiled=True)
    packed = exchange(pack(query_act[0], output_grad[0], key_act[0], value_act[0]))
    packed = packed.reshape(SEQ, PACK)
    e, inverse, dv = attend_probs(packed)
    dv_parts = exchange(dv.reshape(DEVICES, LOCAL, HEAD_DIM))
    dq, dk = attend_grads(packed, e, inverse)
    value_grad = pair_sum(dv_parts).reshape(ROWS, KV_HEADS * HEAD_DIM)
    sections = lax.axis_size("section")
    here = lax.axis_index("section")
    flag = jnp.where(here == sections - 1, 1.0, 0.0).astype(F32).reshape(1)
    term = norm_term(
        value_grad,
        weight,
        layer_input[0].reshape(ROWS, D),
        norm_gain,
        top_grad.reshape(ROWS, D),
        flag,
    )
    terms = lax.all_to_all(term.reshape(sections, ROWS // sections, D), "section", 0, 0, tiled=True)
    run = terms[sections - 1]
    sums = [run]
    for s in range(sections - 2, -1, -1):
        run = (run.astype(F32) + terms[s].astype(F32)).astype(BF)
        sums.append(run)
    sums = jnp.stack(sums[::-1])
    current = lax.all_to_all(sums, "section", 0, 0, tiled=True)
    dq_parts = exchange(dq.reshape(DEVICES, LOCAL, QCOLS))
    dk_parts = exchange(dk.reshape(DEVICES, LOCAL, HEAD_DIM))
    return (
        current.reshape(1, BATCH, LOCAL, D),
        unpack(dq_parts)[None],
        pair_sum(dk_parts)[None],
    )


def solution(mesh):
    return jax.shard_map(
        local,
        mesh=mesh,
        in_specs=(
            P("section", None, "seq", None),
            P("section", None, "seq", None),
            P("section", None, "seq", None),
            P("section", None, "seq", None),
            P("section", None, "seq", None),
            P("section", "seq", None),
            P("section", None),
            P(None, "seq", None),
        ),
        out_specs=(
            P("section", None, "seq", None),
            P("section", None, "seq", None),
            P("section", None, "seq", None),
        ),
        check_vma=False,
    )
```

```python
import jax
import jax.numpy as jnp
from jax import lax
from jax.experimental import pallas as pl
from jax.experimental.pallas import tpu as pltpu
from jax.sharding import PartitionSpec as P

D = 8192
KV_HEADS = 8
HEAD_DIM = 128
BATCH = 2
SEQ = 2048
DEVICES = 32
LOCAL = SEQ // DEVICES
UNIT_HEADS = 4
QCOLS = UNIT_HEADS * HEAD_DIM
UNITS = DEVICES // BATCH
PACK = QCOLS + HEAD_DIM
STEP_UNITS = 4
TOK = 128
BLOCKS = SEQ // TOK
CHUNK = 256
CHUNKS = SEQ // CHUNK
HALF = BLOCKS // 2
HALF_CHUNKS = CHUNKS // 2
HALF = BLOCKS // 2
HALF_CHUNKS = CHUNKS // 2
SCALE = HEAD_DIM ** (-0.5)
LOG2E = 1.4426950408889634
NEG = -1e30

BF = jnp.bfloat16
F32 = jnp.float32
LAST = (((1,), (1,)), ((), ()))


PARAMS = pltpu.CompilerParams(vmem_limit_bytes=60 << 20)


def cost(us):
    return pl.CostEstimate(flops=int(us * 1e9), transcendentals=0, bytes_accessed=0)


def pack_body(wide_ref, slim_ref, out_ref):
    for unit in range(STEP_UNITS):
        cols = slice(unit * QCOLS, (unit + 1) * QCOLS)
        kv = slice(unit // 2 * HEAD_DIM, (unit // 2 + 1) * HEAD_DIM)
        out_ref[unit, :, :QCOLS] = wide_ref[:, cols]
        out_ref[unit, :, QCOLS:] = slim_ref[:, kv]


def pack(wide, slim):
    per_seq = UNITS // STEP_UNITS
    return pl.pallas_call(
        pack_body,
        grid=(BATCH, per_seq),
        out_shape=jax.ShapeDtypeStruct((DEVICES, LOCAL, PACK), BF),
        in_specs=[
            pl.BlockSpec((None, LOCAL, STEP_UNITS * QCOLS), lambda b, i: (b, 0, i)),
            pl.BlockSpec((None, LOCAL, STEP_UNITS // 2 * HEAD_DIM), lambda b, i: (b, 0, i)),
        ],
        out_specs=pl.BlockSpec((STEP_UNITS, LOCAL, PACK), lambda b, i: (b * per_seq + i, 0, 0)),
        cost_estimate=cost(3),
        compiler_params=PARAMS,
        name="pack",
    )(wide, slim)


def unpack_body(in_ref, wide_ref, slim_ref):
    for unit in range(STEP_UNITS):
        wide_ref[:, unit * QCOLS : (unit + 1) * QCOLS] = in_ref[unit, :, :QCOLS]
    for head in range(STEP_UNITS // 2):
        total = in_ref[2 * head, :, QCOLS:].astype(F32) + in_ref[2 * head + 1, :, QCOLS:].astype(F32)
        slim_ref[:, head * HEAD_DIM : (head + 1) * HEAD_DIM] = total.astype(BF)


def unpack(parts):
    per_seq = UNITS // STEP_UNITS
    return pl.pallas_call(
        unpack_body,
        grid=(BATCH, per_seq),
        out_shape=(
            jax.ShapeDtypeStruct((BATCH, LOCAL, D), BF),
            jax.ShapeDtypeStruct((BATCH, LOCAL, KV_HEADS * HEAD_DIM), BF),
        ),
        in_specs=[pl.BlockSpec((STEP_UNITS, LOCAL, PACK), lambda b, i: (b * per_seq + i, 0, 0))],
        out_specs=(
            pl.BlockSpec((None, LOCAL, STEP_UNITS * QCOLS), lambda b, i: (b, 0, i)),
            pl.BlockSpec((None, LOCAL, STEP_UNITS // 2 * HEAD_DIM), lambda b, i: (b, 0, i)),
        ),
        cost_estimate=cost(5),
        compiler_params=PARAMS,
        name="unpack",
    )(parts)


def stack_heads(ref):
    return jnp.concatenate(
        [ref[:, h * HEAD_DIM : (h + 1) * HEAD_DIM] for h in range(UNIT_HEADS)], axis=0
    )


def fold(chunk, op):
    return op(chunk.reshape(CHUNK // 8, 8, QCOLS), axis=0)


def join(a, b, op):
    return b if a is None else op(a, b)


def chunk_rows(c):
    return slice(c * CHUNK, (c + 1) * CHUNK)


def probs_body(q_ref, k_ref, low_ref, high_ref, l_ref, s_ref):
    block = pl.program_id(0)

    for last in range(CHUNKS):
        e_ref = low_ref if last < HALF_CHUNKS else high_ref

        @pl.when(block // 2 == last)
        def _():
            q = stack_heads(q_ref)
            top = None
            for c in range(last + 1):
                s = lax.dot_general(k_ref[chunk_rows(c), :], q, LAST, preferred_element_type=F32)
                if c == last:
                    key_pos = c * CHUNK + lax.broadcasted_iota(jnp.int32, (CHUNK, QCOLS), 0)
                    query_pos = block * TOK + lax.broadcasted_iota(
                        jnp.int32, (CHUNK, QCOLS), 1
                    ) % TOK
                    s = jnp.where(key_pos <= query_pos, s, NEG)
                s_ref[c] = s
                top = join(top, fold(s, jnp.max), jnp.maximum)
            top = jnp.max(top, axis=0, keepdims=True)
            total = None
            for c in range(last + 1):
                e = jnp.exp2((s_ref[c] - top) * (SCALE * LOG2E))
                e_ref[c] = e.astype(BF)
                total = join(total, fold(e, jnp.sum), jnp.add)
            l_ref[...] = 1.0 / jnp.sum(total, axis=0, keepdims=True)


LOW_SPEC = pl.BlockSpec(
    (None, HALF_CHUNKS, CHUNK, QCOLS), lambda t: (jnp.minimum(t, HALF - 1), 0, 0, 0)
)
HIGH_SPEC = pl.BlockSpec(
    (None, CHUNKS, CHUNK, QCOLS), lambda t: (jnp.maximum(t - HALF, 0), 0, 0, 0)
)
STAT_SPEC = pl.BlockSpec((None, 1, QCOLS), lambda t: (t, 0, 0))


def attend_probs(packed):
    return pl.pallas_call(
        probs_body,
        grid=(BLOCKS,),
        out_shape=(
            jax.ShapeDtypeStruct((HALF, HALF_CHUNKS, CHUNK, QCOLS), BF),
            jax.ShapeDtypeStruct((HALF, CHUNKS, CHUNK, QCOLS), BF),
            jax.ShapeDtypeStruct((BLOCKS, 1, QCOLS), F32),
        ),
        in_specs=[
            pl.BlockSpec((TOK, QCOLS), lambda t: (t, 0)),
            pl.BlockSpec((SEQ, HEAD_DIM), lambda t: (0, UNIT_HEADS)),
        ],
        out_specs=(LOW_SPEC, HIGH_SPEC, STAT_SPEC),
        scratch_shapes=[pltpu.VMEM((CHUNKS, CHUNK, QCOLS), F32)],
        compiler_params=PARAMS,
        cost_estimate=cost(18),
        name="probs",
    )(packed, packed)


def scaled_grad(g_ref, l_ref):
    column = jnp.transpose(jnp.broadcast_to(l_ref[...], (HEAD_DIM, QCOLS)))
    return (stack_heads(g_ref).astype(F32) * column).astype(BF)


def values_body(g_ref, low_ref, high_ref, l_ref, dv_ref, acc):
    block = pl.program_id(0)

    @pl.when(block == 0)
    def _():
        acc[...] = jnp.zeros_like(acc)

    for last in range(CHUNKS):
        e_ref = low_ref if last < HALF_CHUNKS else high_ref

        @pl.when(block // 2 == last)
        def _():
            g = scaled_grad(g_ref, l_ref)
            for c in range(last + 1):
                acc[chunk_rows(c), :] += jnp.dot(e_ref[c], g, preferred_element_type=F32)

    @pl.when(block == BLOCKS - 1)
    def _():
        dv_ref[...] = acc[...].astype(BF)


def attend_values(packed, low, high, inverse):
    return pl.pallas_call(
        values_body,
        grid=(BLOCKS,),
        out_shape=jax.ShapeDtypeStruct((SEQ, HEAD_DIM), BF),
        in_specs=[
            pl.BlockSpec((TOK, QCOLS), lambda t: (t, 0)),
            LOW_SPEC,
            HIGH_SPEC,
            STAT_SPEC,
        ],
        out_specs=pl.BlockSpec((SEQ, HEAD_DIM), lambda t: (0, 0)),
        scratch_shapes=[pltpu.VMEM((SEQ, HEAD_DIM), F32)],
        compiler_params=PARAMS,
        cost_estimate=cost(10),
        name="values",
    )(packed, low, high, inverse)


def grads_body(
    q_ref, g_ref, k_ref, v_ref, low_ref, high_ref, l_ref, out_ref, p_ref, kt_ref, acc
):
    step = pl.program_id(0)
    block = BLOCKS - 1 - step

    @pl.when(step == 0)
    def _():
        acc[...] = jnp.zeros_like(acc)
        for c in range(CHUNKS):
            kt_ref[c] = jnp.transpose(k_ref[chunk_rows(c), :])

    for last in range(CHUNKS):
        e_ref = low_ref if last < HALF_CHUNKS else high_ref

        @pl.when(block // 2 == last)
        def _():
            q = stack_heads(q_ref)
            g = scaled_grad(g_ref, l_ref)
            total = None
            for c in range(last + 1):
                p = lax.dot_general(v_ref[chunk_rows(c), :], g, LAST, preferred_element_type=F32)
                p_ref[c] = p
                total = join(total, fold(p * e_ref[c].astype(F32), jnp.sum), jnp.add)
            center = jnp.sum(total, axis=0, keepdims=True) * l_ref[...]
            dq = None
            for c in range(last + 1):
                ds = (e_ref[c].astype(F32) * (p_ref[c] - center)).astype(BF)
                acc[chunk_rows(c), :] += jnp.dot(ds, q, preferred_element_type=F32)
                dq = join(dq, jnp.dot(kt_ref[c], ds, preferred_element_type=F32), jnp.add)
            dq = dq * SCALE
            for h in range(UNIT_HEADS):
                cols = slice(h * HEAD_DIM, (h + 1) * HEAD_DIM)
                out_ref[:, cols] = jnp.transpose(dq[:, cols]).astype(BF)

    rows = pl.ds(pl.multiple_of(block * TOK, TOK), TOK)
    out_ref[:, QCOLS:] = (acc[rows, :] * SCALE).astype(BF)


def backward(spec):
    index = spec.index_map
    return pl.BlockSpec(spec.block_shape, lambda t: index(BLOCKS - 1 - t))


def attend_grads(query_key, grad_value, low, high, inverse):
    wide = backward(pl.BlockSpec((TOK, QCOLS), lambda t: (t, 0)))
    slim = pl.BlockSpec((SEQ, HEAD_DIM), lambda t: (0, UNIT_HEADS))
    return pl.pallas_call(
        grads_body,
        grid=(BLOCKS,),
        out_shape=jax.ShapeDtypeStruct((SEQ, PACK), BF),
        in_specs=[wide, wide, slim, slim]
        + [backward(LOW_SPEC), backward(HIGH_SPEC), backward(STAT_SPEC)],
        out_specs=backward(pl.BlockSpec((TOK, PACK), lambda t: (t, 0))),
        scratch_shapes=[
            pltpu.VMEM((CHUNKS, CHUNK, QCOLS), F32),
            pltpu.VMEM((CHUNKS, HEAD_DIM, CHUNK), BF),
            pltpu.VMEM((SEQ, HEAD_DIM), F32),
        ],
        compiler_params=PARAMS,
        cost_estimate=cost(27),
        name="grads",
    )(query_key, grad_value, query_key, grad_value, low, high, inverse)


ROWS = BATCH * LOCAL
FEATS = 1024
SECTIONS = 4
PART = ROWS // SECTIONS


def pair_sums(parts_ref, emit):
    for seq in range(BATCH):
        for head in range(KV_HEADS):
            first = seq * UNITS + 2 * head
            total = parts_ref[first].astype(F32) + parts_ref[first + 1].astype(F32)
            emit(seq, slice(head * HEAD_DIM, (head + 1) * HEAD_DIM), total.astype(BF))


def term_body(here_ref, parts_ref, w_ref, x_ref, gain_ref, top_ref, *refs):
    out_refs, (vg_ref, u_ref, xs_ref, acc) = refs[:SECTIONS], refs[SECTIONS:]
    step = pl.program_id(0)

    @pl.when(step == 0)
    def _():
        acc[...] = jnp.zeros_like(acc)

        def emit(seq, cols, value):
            vg_ref[seq * LOCAL : (seq + 1) * LOCAL, cols] = value

        pair_sums(parts_ref, emit)

    u = lax.dot_general(vg_ref[...], w_ref[...], LAST, preferred_element_type=F32) * gain_ref[...]
    x = x_ref[...].astype(F32)
    u_ref[step] = u
    acc[0] += jnp.sum(x * x, axis=1, keepdims=True)
    acc[1] += jnp.sum(x * u, axis=1, keepdims=True)
    xs_ref[step] = x_ref[...]

    @pl.when(step == pl.num_programs(0) - 1)
    def _():
        here = here_ref[0]
        flag = jnp.where(here == SECTIONS - 1, 1.0, 0.0).astype(F32)
        r = lax.rsqrt(acc[0] * (1.0 / D) + 1e-05)
        inner = acc[1] * (1.0 / D) * (r * r * r)
        acc[0] = r
        acc[1] = inner
        for k in range(SECTIONS):
            rows = pl.ds(pl.multiple_of(((here + k) % SECTIONS) * PART, PART), PART)
            r = acc[0, rows, :]
            inner = acc[1, rows, :]
            for i in range(D // FEATS):
                cols = slice(i * FEATS, (i + 1) * FEATS)
                term = r * u_ref[i, rows, :] - xs_ref[i, rows, :].astype(F32) * inner
                term = term + top_ref[rows, cols].astype(F32) * flag
                out_refs[k][:, cols] = term.astype(BF)


def norm_term(here, parts, weight, x, gain, top):
    steps = D // FEATS
    return pl.pallas_call(
        term_body,
        grid=(steps,),
        out_shape=tuple(jax.ShapeDtypeStruct((PART, D), BF) for _ in range(SECTIONS)),
        in_specs=[
            pl.BlockSpec(memory_space=pltpu.SMEM),
            pl.BlockSpec((DEVICES, LOCAL, HEAD_DIM), lambda i: (0, 0, 0)),
            pl.BlockSpec((FEATS, KV_HEADS * HEAD_DIM), lambda i: (i, 0)),
            pl.BlockSpec((ROWS, FEATS), lambda i: (0, i)),
            pl.BlockSpec((1, FEATS), lambda i: (0, i)),
            pl.BlockSpec((ROWS, D), lambda i: (0, 0)),
        ],
        out_specs=tuple(pl.BlockSpec((PART, D), lambda i: (0, 0)) for _ in range(SECTIONS)),
        scratch_shapes=[
            pltpu.VMEM((ROWS, KV_HEADS * HEAD_DIM), BF),
            pltpu.VMEM((steps, ROWS, FEATS), F32),
            pltpu.VMEM((steps, ROWS, FEATS), BF),
            pltpu.VMEM((2, ROWS, 1), F32),
        ],
        compiler_params=PARAMS,
        cost_estimate=cost(12),
        name="term",
    )(here, parts, weight, x, gain, top)


def sums_body(here_ref, *refs):
    parts, outs = refs[:SECTIONS], refs[SECTIONS:]
    here = here_ref[0]
    place = [(here - j) % SECTIONS for j in range(SECTIONS)]
    values = [part[...].astype(F32) for part in parts]
    for k in range(SECTIONS):
        total = values[k]
        for j in range(SECTIONS):
            if j != k:
                total = total + values[j] * jnp.where(place[j] > place[k], 1.0, 0.0).astype(F32)
        outs[k][...] = total.astype(BF)


def suffix_sums(here, parts):
    cols = D // 4
    spec = pl.BlockSpec((PART, cols), lambda i: (0, i))
    return pl.pallas_call(
        sums_body,
        grid=(D // cols,),
        out_shape=tuple(jax.ShapeDtypeStruct((PART, D), BF) for _ in range(SECTIONS)),
        in_specs=[pl.BlockSpec(memory_space=pltpu.SMEM)] + [spec] * SECTIONS,
        out_specs=(spec,) * SECTIONS,
        cost_estimate=cost(2),
        compiler_params=PARAMS,
        name="suffix_sums",
    )(here, *parts)


def place_body(here_ref, *refs):
    parts, out_ref = refs[:SECTIONS], refs[SECTIONS]
    here = here_ref[0]
    for k in range(SECTIONS):
        rows = pl.ds(pl.multiple_of(((here + k) % SECTIONS) * PART, PART), PART)
        out_ref[rows, :] = parts[k][...]


def place(here, parts):
    cols = D // 4
    spec = pl.BlockSpec((PART, cols), lambda i: (0, i))
    return pl.pallas_call(
        place_body,
        grid=(D // cols,),
        out_shape=jax.ShapeDtypeStruct((ROWS, D), BF),
        in_specs=[pl.BlockSpec(memory_space=pltpu.SMEM)] + [spec] * SECTIONS,
        out_specs=pl.BlockSpec((ROWS, cols), lambda i: (0, i)),
        cost_estimate=cost(2),
        compiler_params=PARAMS,
        name="place",
    )(here, *parts)


def exchange(parts):
    return lax.all_to_all(parts, "seq", 0, 0, tiled=True)


def turn(array, by):
    pairs = [(i, (i + by) % SECTIONS) for i in range(SECTIONS)]
    return lax.ppermute(array, "section", pairs)


def local(
    layer_input, query_act, key_act, value_act, output_grad, value_weight, norm_gain, top_grad
):
    weight = lax.all_gather(value_weight[0], "seq", axis=0, tiled=True)
    query_key = exchange(pack(query_act[0], key_act[0])).reshape(SEQ, PACK)
    grad_value = exchange(pack(output_grad[0], value_act[0])).reshape(SEQ, PACK)
    low, high, inverse = attend_probs(query_key)
    dv = attend_values(grad_value, low, high, inverse)
    dv_parts = exchange(dv.reshape(DEVICES, LOCAL, HEAD_DIM))
    grads = attend_grads(query_key, grad_value, low, high, inverse)
    grads_back = exchange(grads.reshape(DEVICES, LOCAL, PACK))
    here = lax.axis_index("section").astype(jnp.int32).reshape(1)
    terms = norm_term(
        here,
        dv_parts,
        weight,
        layer_input[0].reshape(ROWS, D),
        norm_gain,
        top_grad.reshape(ROWS, D),
    )
    arrived = [terms[0]] + [turn(terms[k], k) for k in range(1, SECTIONS)]
    sums = suffix_sums(here, arrived)
    back = [sums[0]] + [turn(sums[k], -k) for k in range(1, SECTIONS)]
    current = place(here, back)
    query_grad, key_grad = unpack(grads_back)
    return current.reshape(1, BATCH, LOCAL, D), query_grad[None], key_grad[None]


def solution(mesh):
    return jax.shard_map(
        local,
        mesh=mesh,
        in_specs=(
            P("section", None, "seq", None),
            P("section", None, "seq", None),
            P("section", None, "seq", None),
            P("section", None, "seq", None),
            P("section", None, "seq", None),
            P("section", "seq", None),
            P("section", None),
            P(None, "seq", None),
        ),
        out_specs=(
            P("section", None, "seq", None),
            P("section", None, "seq", None),
            P("section", None, "seq", None),
        ),
        check_vma=False,
    )
```

```python
import jax
import jax.numpy as jnp
from jax import lax
from jax.experimental import pallas as pl
from jax.experimental.pallas import tpu as pltpu
from jax.sharding import PartitionSpec as P

D = 8192
KV_HEADS = 8
HEAD_DIM = 128
BATCH = 2
SEQ = 2048
DEVICES = 32
LOCAL = SEQ // DEVICES
UNIT_HEADS = 4
QCOLS = UNIT_HEADS * HEAD_DIM
UNITS = DEVICES // BATCH
PACK = QCOLS + HEAD_DIM
STEP_UNITS = 4
TOK = 128
BLOCKS = SEQ // TOK
CHUNK = 256
CHUNKS = SEQ // CHUNK
HALF = BLOCKS // 2
SIDES = 2
STEPS = BLOCKS // SIDES
HALF_CHUNKS = CHUNKS // 2
SCALE = HEAD_DIM ** (-0.5)
LOG2E = 1.4426950408889634
NEG = -1e30

BF = jnp.bfloat16
F32 = jnp.float32
LAST = (((1,), (1,)), ((), ()))


PARAMS = pltpu.CompilerParams(vmem_limit_bytes=60 << 20)


def cost(us):
    return pl.CostEstimate(flops=int(us * 1e9), transcendentals=0, bytes_accessed=0)


def pack_body(q_ref, g_ref, k_ref, v_ref, out_ref):
    for unit in range(STEP_UNITS):
        cols = slice(unit * QCOLS, (unit + 1) * QCOLS)
        kv = slice(unit // 2 * HEAD_DIM, (unit // 2 + 1) * HEAD_DIM)
        out_ref[unit, :, :QCOLS] = q_ref[:, cols]
        out_ref[unit, :, QCOLS : 2 * QCOLS] = g_ref[:, cols]
        out_ref[unit, :, 2 * QCOLS : 2 * QCOLS + HEAD_DIM] = k_ref[:, kv]
        out_ref[unit, :, 2 * QCOLS + HEAD_DIM :] = v_ref[:, kv]


def pack(q, g, k, v):
    wide = pl.BlockSpec((None, LOCAL, STEP_UNITS * QCOLS), lambda b, i: (b, 0, i))
    slim = pl.BlockSpec((None, LOCAL, STEP_UNITS // 2 * HEAD_DIM), lambda b, i: (b, 0, i))
    per_seq = UNITS // STEP_UNITS
    return pl.pallas_call(
        pack_body,
        grid=(BATCH, per_seq),
        out_shape=jax.ShapeDtypeStruct((DEVICES, LOCAL, 2 * PACK), BF),
        in_specs=[wide, wide, slim, slim],
        out_specs=pl.BlockSpec(
            (STEP_UNITS, LOCAL, 2 * PACK), lambda b, i: (b * per_seq + i, 0, 0)
        ),
        compiler_params=PARAMS,
        cost_estimate=cost(6),
        name="pack",
    )(q, g, k, v)


def unpack_body(in_ref, wide_ref, slim_ref):
    for unit in range(STEP_UNITS):
        wide_ref[:, unit * QCOLS : (unit + 1) * QCOLS] = in_ref[unit, :, :QCOLS]
    for head in range(STEP_UNITS // 2):
        total = in_ref[2 * head, :, QCOLS:].astype(F32) + in_ref[2 * head + 1, :, QCOLS:].astype(F32)
        slim_ref[:, head * HEAD_DIM : (head + 1) * HEAD_DIM] = total.astype(BF)


def unpack(parts):
    per_seq = UNITS // STEP_UNITS
    return pl.pallas_call(
        unpack_body,
        grid=(BATCH, per_seq),
        out_shape=(
            jax.ShapeDtypeStruct((BATCH, LOCAL, D), BF),
            jax.ShapeDtypeStruct((BATCH, LOCAL, KV_HEADS * HEAD_DIM), BF),
        ),
        in_specs=[pl.BlockSpec((STEP_UNITS, LOCAL, PACK), lambda b, i: (b * per_seq + i, 0, 0))],
        out_specs=(
            pl.BlockSpec((None, LOCAL, STEP_UNITS * QCOLS), lambda b, i: (b, 0, i)),
            pl.BlockSpec((None, LOCAL, STEP_UNITS // 2 * HEAD_DIM), lambda b, i: (b, 0, i)),
        ),
        cost_estimate=cost(5),
        compiler_params=PARAMS,
        name="unpack",
    )(parts)


def stack_heads(ref, side):
    rows = slice(side * TOK, (side + 1) * TOK)
    return jnp.concatenate(
        [ref[rows, h * HEAD_DIM : (h + 1) * HEAD_DIM] for h in range(UNIT_HEADS)], axis=0
    )


def fold(chunk, op):
    return op(chunk.reshape(CHUNK // 8, 8, QCOLS), axis=0)


def join(a, b, op):
    return b if a is None else op(a, b)


def chunk_rows(c):
    return slice(c * CHUNK, (c + 1) * CHUNK)


def score_chunk(q, k_ref, s_ref, block, last, top, c):
    s = lax.dot_general(k_ref[chunk_rows(c), :], q, LAST, preferred_element_type=F32)
    if c == last:
        key_pos = c * CHUNK + lax.broadcasted_iota(jnp.int32, (CHUNK, QCOLS), 0)
        query_pos = block * TOK + lax.broadcasted_iota(jnp.int32, (CHUNK, QCOLS), 1) % TOK
        s = jnp.where(key_pos <= query_pos, s, NEG)
    s_ref[c] = s
    return join(top, fold(s, jnp.max), jnp.maximum)


def scaled_grad(g, inverse):
    column = jnp.transpose(jnp.broadcast_to(inverse, (HEAD_DIM, QCOLS)))
    return (g.astype(F32) * column).astype(BF)


def probs_body(q_ref, g_ref, k_ref, low_ref, high_ref, l_ref, dv_ref, s_ref, acc):
    step = pl.program_id(0)

    @pl.when(step == 0)
    def _():
        acc[...] = jnp.zeros_like(acc)

    for last in range(CHUNKS):
        e_ref = low_ref if last < HALF_CHUNKS else high_ref

        @pl.when(step * SIDES // 2 == last)
        def _():
            tops = []
            for side in range(SIDES):
                q = stack_heads(q_ref, side)
                top = None
                for c in range(last + 1):
                    block = step * SIDES + side
                    top = score_chunk(q, k_ref, s_ref.at[side], block, last, top, c)
                tops.append(jnp.max(top, axis=0, keepdims=True))
            grads = []
            for side in range(SIDES):
                total = None
                for c in range(last + 1):
                    e = jnp.exp2((s_ref[side, c] - tops[side]) * (SCALE * LOG2E))
                    e_ref[side, c] = e.astype(BF)
                    total = join(total, fold(e, jnp.sum), jnp.add)
                inverse = 1.0 / jnp.sum(total, axis=0, keepdims=True)
                l_ref[side] = inverse
                grads.append(scaled_grad(stack_heads(g_ref, side), inverse))
            for c in range(last + 1):
                total = None
                for side in range(SIDES):
                    part = jnp.dot(e_ref[side, c], grads[side], preferred_element_type=F32)
                    total = join(total, part, jnp.add)
                acc[chunk_rows(c), :] += total

    @pl.when(step == STEPS - 1)
    def _():
        dv_ref[...] = acc[...].astype(BF)


LOW_SPEC = pl.BlockSpec(
    (SIDES, HALF_CHUNKS, CHUNK, QCOLS), lambda t: (jnp.minimum(t, STEPS // 2 - 1), 0, 0, 0)
)
HIGH_SPEC = pl.BlockSpec(
    (SIDES, CHUNKS, CHUNK, QCOLS), lambda t: (jnp.maximum(t - STEPS // 2, 0), 0, 0, 0)
)
STAT_SPEC = pl.BlockSpec((SIDES, 1, QCOLS), lambda t: (t, 0, 0))
Q_SPEC = pl.BlockSpec((SIDES * TOK, QCOLS), lambda t: (t, 0))
G_SPEC = pl.BlockSpec((SIDES * TOK, QCOLS), lambda t: (t, 1))
K_SPEC = pl.BlockSpec((SEQ, HEAD_DIM), lambda t: (0, 2 * UNIT_HEADS))
V_SPEC = pl.BlockSpec((SEQ, HEAD_DIM), lambda t: (0, 2 * UNIT_HEADS + 1))


def attend_probs(packed):
    return pl.pallas_call(
        probs_body,
        grid=(STEPS,),
        out_shape=(
            jax.ShapeDtypeStruct((HALF, HALF_CHUNKS, CHUNK, QCOLS), BF),
            jax.ShapeDtypeStruct((HALF, CHUNKS, CHUNK, QCOLS), BF),
            jax.ShapeDtypeStruct((BLOCKS, 1, QCOLS), F32),
            jax.ShapeDtypeStruct((SEQ, HEAD_DIM), BF),
        ),
        in_specs=[Q_SPEC, G_SPEC, K_SPEC],
        out_specs=(
            LOW_SPEC,
            HIGH_SPEC,
            STAT_SPEC,
            pl.BlockSpec((SEQ, HEAD_DIM), lambda t: (0, 0)),
        ),
        scratch_shapes=[
            pltpu.VMEM((SIDES, CHUNKS, CHUNK, QCOLS), F32),
            pltpu.VMEM((SEQ, HEAD_DIM), F32),
        ],
        compiler_params=PARAMS,
        cost_estimate=cost(27),
        name="probs",
    )(packed, packed, packed)


def grads_body(
    q_ref, g_ref, k_ref, v_ref, low_ref, high_ref, l_ref, out_ref, p_ref, kt_ref, acc
):
    step = pl.program_id(0)
    place = STEPS - 1 - step

    @pl.when(step == 0)
    def _():
        acc[...] = jnp.zeros_like(acc)
        for c in range(CHUNKS):
            kt_ref[c] = jnp.transpose(k_ref[chunk_rows(c), :])

    for last in range(CHUNKS):
        e_ref = low_ref if last < HALF_CHUNKS else high_ref

        @pl.when(place * SIDES // 2 == last)
        def _():
            centers = []
            for side in range(SIDES):
                g = scaled_grad(stack_heads(g_ref, side), l_ref[side])
                total = None
                for c in range(last + 1):
                    p = lax.dot_general(
                        v_ref[chunk_rows(c), :], g, LAST, preferred_element_type=F32
                    )
                    p_ref[side, c] = p
                    total = join(total, fold(p * e_ref[side, c].astype(F32), jnp.sum), jnp.add)
                centers.append(jnp.sum(total, axis=0, keepdims=True) * l_ref[side])
            queries = [stack_heads(q_ref, side) for side in range(SIDES)]
            dqs = [None] * SIDES
            for c in range(last + 1):
                dk = None
                for side in range(SIDES):
                    ds = e_ref[side, c].astype(F32) * (p_ref[side, c] - centers[side])
                    ds = ds.astype(BF)
                    part = jnp.dot(ds, queries[side], preferred_element_type=F32)
                    dk = join(dk, part, jnp.add)
                    part = jnp.dot(kt_ref[c], ds, preferred_element_type=F32)
                    dqs[side] = join(dqs[side], part, jnp.add)
                acc[chunk_rows(c), :] += dk
            for side in range(SIDES):
                dq = dqs[side] * SCALE
                for h in range(UNIT_HEADS):
                    cols = slice(h * HEAD_DIM, (h + 1) * HEAD_DIM)
                    out_ref[side * TOK : (side + 1) * TOK, cols] = jnp.transpose(
                        dq[:, cols]
                    ).astype(BF)

    rows = pl.ds(pl.multiple_of(place * SIDES * TOK, SIDES * TOK), SIDES * TOK)
    out_ref[:, QCOLS:] = (acc[rows, :] * SCALE).astype(BF)


def backward(spec):
    index = spec.index_map
    return pl.BlockSpec(spec.block_shape, lambda t: index(STEPS - 1 - t))


def attend_grads(packed, low, high, inverse):
    return pl.pallas_call(
        grads_body,
        grid=(STEPS,),
        out_shape=jax.ShapeDtypeStruct((SEQ, PACK), BF),
        in_specs=[backward(Q_SPEC), backward(G_SPEC), K_SPEC, V_SPEC]
        + [backward(LOW_SPEC), backward(HIGH_SPEC), backward(STAT_SPEC)],
        out_specs=backward(pl.BlockSpec((SIDES * TOK, PACK), lambda t: (t, 0))),
        scratch_shapes=[
            pltpu.VMEM((SIDES, CHUNKS, CHUNK, QCOLS), F32),
            pltpu.VMEM((CHUNKS, HEAD_DIM, CHUNK), BF),
            pltpu.VMEM((SEQ, HEAD_DIM), F32),
        ],
        compiler_params=PARAMS,
        cost_estimate=cost(27),
        name="grads",
    )(packed, packed, packed, packed, low, high, inverse)


ROWS = BATCH * LOCAL
FEATS = D // DEVICES
PIECES = 4
SECTIONS = 4
PART = ROWS // SECTIONS


def pair_sums(parts_ref, emit):
    for seq in range(BATCH):
        for head in range(KV_HEADS):
            first = seq * UNITS + 2 * head
            total = parts_ref[first].astype(F32) + parts_ref[first + 1].astype(F32)
            emit(seq, slice(head * HEAD_DIM, (head + 1) * HEAD_DIM), total.astype(BF))


def term_body(place_ref, parts_ref, own_ref, other_ref, x_ref, gain_ref, top_ref, *refs):
    out_refs, (vg_ref, u_ref, xs_ref, acc) = refs[:SECTIONS], refs[SECTIONS:]
    step = pl.program_id(0)
    here, core = place_ref[0], place_ref[1]

    @pl.when(step == 0)
    def _():
        acc[...] = jnp.zeros_like(acc)

        def emit(seq, cols, value):
            vg_ref[seq * LOCAL : (seq + 1) * LOCAL, cols] = value

        pair_sums(parts_ref, emit)

    for weight_ref, parity in ((own_ref, core), (other_ref, 1 - core)):
        u = lax.dot_general(vg_ref[...], weight_ref[...], LAST, preferred_element_type=F32)
        for i in range(PIECES // 2):
            u_ref[step * PIECES + 2 * i + parity] = u[:, i * FEATS : (i + 1) * FEATS]
    squares = jnp.zeros((ROWS, 1), F32)
    inner = jnp.zeros((ROWS, 1), F32)
    for i in range(PIECES):
        cols = slice(i * FEATS, (i + 1) * FEATS)
        x = x_ref[:, cols].astype(F32)
        u = u_ref[step * PIECES + i] * gain_ref[:, cols]
        u_ref[step * PIECES + i] = u
        xs_ref[step * PIECES + i] = x_ref[:, cols]
        squares = squares + jnp.sum(x * x, axis=1, keepdims=True)
        inner = inner + jnp.sum(x * u, axis=1, keepdims=True)
    acc[0] += squares
    acc[1] += inner

    @pl.when(step == pl.num_programs(0) - 1)
    def _():
        flag = jnp.where(here == SECTIONS - 1, 1.0, 0.0).astype(F32)
        r = lax.rsqrt(acc[0] * (1.0 / D) + 1e-05)
        acc[1] = acc[1] * (1.0 / D) * (r * r * r)
        acc[0] = r
        for k in range(SECTIONS):
            rows = pl.ds(pl.multiple_of(((here + k) % SECTIONS) * PART, PART), PART)
            r = acc[0, rows, :]
            inner = acc[1, rows, :]
            for i in range(D // FEATS):
                cols = slice(i * FEATS, (i + 1) * FEATS)
                term = r * u_ref[i, rows, :] - xs_ref[i, rows, :].astype(F32) * inner
                term = term + top_ref[rows, cols].astype(F32) * flag
                out_refs[k][:, cols] = term.astype(BF)


def norm_term(place, parts, own, other, x, gain, top):
    width = PIECES * FEATS
    weight = pl.BlockSpec((width // 2, KV_HEADS * HEAD_DIM), lambda i: (i, 0))
    return pl.pallas_call(
        term_body,
        grid=(D // width,),
        out_shape=tuple(jax.ShapeDtypeStruct((PART, D), BF) for _ in range(SECTIONS)),
        in_specs=[
            pl.BlockSpec(memory_space=pltpu.SMEM),
            pl.BlockSpec((DEVICES, LOCAL, HEAD_DIM), lambda i: (0, 0, 0)),
            weight,
            weight,
            pl.BlockSpec((ROWS, width), lambda i: (0, i)),
            pl.BlockSpec((1, width), lambda i: (0, i)),
            pl.BlockSpec((ROWS, D), lambda i: (0, 0)),
        ],
        out_specs=tuple(pl.BlockSpec((PART, D), lambda i: (0, 0)) for _ in range(SECTIONS)),
        scratch_shapes=[
            pltpu.VMEM((ROWS, KV_HEADS * HEAD_DIM), BF),
            pltpu.VMEM((D // FEATS, ROWS, FEATS), F32),
            pltpu.VMEM((D // FEATS, ROWS, FEATS), BF),
            pltpu.VMEM((2, ROWS, 1), F32),
        ],
        compiler_params=PARAMS,
        cost_estimate=cost(12),
        name="term",
    )(place, parts, own, other, x, gain, top)


def sums_body(here_ref, *refs):
    parts, outs = refs[:SECTIONS], refs[SECTIONS:]
    here = here_ref[0]
    place = [(here - j) % SECTIONS for j in range(SECTIONS)]
    values = [part[...].astype(F32) for part in parts]
    for k in range(SECTIONS):
        total = values[k]
        for j in range(SECTIONS):
            if j != k:
                total = total + values[j] * jnp.where(place[j] > place[k], 1.0, 0.0).astype(F32)
        outs[k][...] = total.astype(BF)


def suffix_sums(here, parts):
    cols = D // 4
    spec = pl.BlockSpec((PART, cols), lambda i: (0, i))
    return pl.pallas_call(
        sums_body,
        grid=(D // cols,),
        out_shape=tuple(jax.ShapeDtypeStruct((PART, D), BF) for _ in range(SECTIONS)),
        in_specs=[pl.BlockSpec(memory_space=pltpu.SMEM)] + [spec] * SECTIONS,
        out_specs=(spec,) * SECTIONS,
        cost_estimate=cost(2),
        compiler_params=PARAMS,
        name="suffix_sums",
    )(here, *parts)


def place_body(here_ref, *refs):
    parts, out_ref = refs[:SECTIONS], refs[SECTIONS]
    here = here_ref[0]
    for k in range(SECTIONS):
        rows = pl.ds(pl.multiple_of(((here + k) % SECTIONS) * PART, PART), PART)
        out_ref[rows, :] = parts[k][...]


def place(here, parts):
    cols = D // 4
    spec = pl.BlockSpec((PART, cols), lambda i: (0, i))
    return pl.pallas_call(
        place_body,
        grid=(D // cols,),
        out_shape=jax.ShapeDtypeStruct((ROWS, D), BF),
        in_specs=[pl.BlockSpec(memory_space=pltpu.SMEM)] + [spec] * SECTIONS,
        out_specs=pl.BlockSpec((ROWS, cols), lambda i: (0, i)),
        cost_estimate=cost(2),
        compiler_params=PARAMS,
        name="place",
    )(here, *parts)


def exchange(parts):
    return lax.all_to_all(parts, "seq", 0, 0, tiled=True)


def turn(array, by):
    pairs = [(i, (i + by) % SECTIONS) for i in range(SECTIONS)]
    return lax.ppermute(array, "section", pairs)


def local(
    layer_input, query_act, key_act, value_act, output_grad, value_weight, norm_gain, top_grad
):
    cores = [[2 * chip + core for chip in range(DEVICES // 2)] for core in range(2)]
    own = lax.all_gather(value_weight[0], "seq", axis=0, tiled=True, axis_index_groups=cores)
    packed = exchange(pack(query_act[0], output_grad[0], key_act[0], value_act[0]))
    packed = packed.reshape(SEQ, 2 * PACK)
    low, high, inverse, dv = attend_probs(packed)
    own, dv = lax.optimization_barrier((own, dv))
    other = lax.ppermute(own, "seq", [(i, i ^ 1) for i in range(DEVICES)])
    dv_parts = exchange(dv.reshape(DEVICES, LOCAL, HEAD_DIM))
    grads = attend_grads(packed, low, high, inverse)
    here = lax.axis_index("section").astype(jnp.int32).reshape(1)
    core = lax.axis_index("seq").astype(jnp.int32).reshape(1) % 2
    terms = norm_term(
        jnp.concatenate([here, core]),
        dv_parts,
        own,
        other,
        layer_input[0].reshape(ROWS, D),
        norm_gain,
        top_grad.reshape(ROWS, D),
    )
    terms, grads = lax.optimization_barrier((terms, grads))
    grads_back = exchange(grads.reshape(DEVICES, LOCAL, PACK))
    arrived = [terms[0]] + [turn(terms[k], k) for k in range(1, SECTIONS)]
    sums = suffix_sums(here, arrived)
    back = [sums[0]] + [turn(sums[k], -k) for k in range(1, SECTIONS)]
    current = place(here, back)
    query_grad, key_grad = unpack(grads_back)
    return current.reshape(1, BATCH, LOCAL, D), query_grad[None], key_grad[None]


def solution(mesh):
    return jax.shard_map(
        local,
        mesh=mesh,
        in_specs=(
            P("section", None, "seq", None),
            P("section", None, "seq", None),
            P("section", None, "seq", None),
            P("section", None, "seq", None),
            P("section", None, "seq", None),
            P("section", "seq", None),
            P("section", None),
            P(None, "seq", None),
        ),
        out_specs=(
            P("section", None, "seq", None),
            P("section", None, "seq", None),
            P("section", None, "seq", None),
        ),
        check_vma=False,
    )
```

```python
import jax
import jax.numpy as jnp
from jax import lax
from jax.experimental import pallas as pl
from jax.experimental.pallas import tpu as pltpu
from jax.sharding import PartitionSpec as P

D = 8192
KV_HEADS = 8
HEAD_DIM = 128
BATCH = 2
SEQ = 2048
DEVICES = 32
LOCAL = SEQ // DEVICES
UNIT_HEADS = 4
QCOLS = UNIT_HEADS * HEAD_DIM
UNITS = DEVICES // BATCH
PACK = QCOLS + HEAD_DIM
STEP_UNITS = 8
TOK = 128
BLOCKS = SEQ // TOK
CHUNK = 256
CHUNKS = SEQ // CHUNK
HALF = BLOCKS // 2
SIDES = 2
STEPS = BLOCKS // SIDES
HALF_CHUNKS = CHUNKS // 2
SCALE = HEAD_DIM ** (-0.5)
LOG2E = 1.4426950408889634
NEG = -1e30

BF = jnp.bfloat16
F32 = jnp.float32
LAST = (((1,), (1,)), ((), ()))


PARAMS = pltpu.CompilerParams(vmem_limit_bytes=60 << 20)


def cost(us):
    return pl.CostEstimate(flops=int(us * 1e9), transcendentals=0, bytes_accessed=0)


def pack_body(q_ref, g_ref, k_ref, v_ref, out_ref):
    for unit in range(STEP_UNITS):
        cols = slice(unit * QCOLS, (unit + 1) * QCOLS)
        kv = slice(unit // 2 * HEAD_DIM, (unit // 2 + 1) * HEAD_DIM)
        out_ref[unit, :, :QCOLS] = q_ref[:, cols]
        out_ref[unit, :, QCOLS : 2 * QCOLS] = g_ref[:, cols]
        out_ref[unit, :, 2 * QCOLS : 2 * QCOLS + HEAD_DIM] = k_ref[:, kv]
        out_ref[unit, :, 2 * QCOLS + HEAD_DIM :] = v_ref[:, kv]


def pack(q, g, k, v):
    wide = pl.BlockSpec((None, LOCAL, STEP_UNITS * QCOLS), lambda b, i: (b, 0, i))
    slim = pl.BlockSpec((None, LOCAL, STEP_UNITS // 2 * HEAD_DIM), lambda b, i: (b, 0, i))
    per_seq = UNITS // STEP_UNITS
    return pl.pallas_call(
        pack_body,
        grid=(BATCH, per_seq),
        out_shape=jax.ShapeDtypeStruct((DEVICES, LOCAL, 2 * PACK), BF),
        in_specs=[wide, wide, slim, slim],
        out_specs=pl.BlockSpec(
            (STEP_UNITS, LOCAL, 2 * PACK), lambda b, i: (b * per_seq + i, 0, 0)
        ),
        compiler_params=PARAMS,
        cost_estimate=cost(6),
        name="pack",
    )(q, g, k, v)


def unpack_body(in_ref, wide_ref, slim_ref):
    for unit in range(STEP_UNITS):
        wide_ref[:, unit * QCOLS : (unit + 1) * QCOLS] = in_ref[unit, :, :QCOLS]
    for head in range(STEP_UNITS // 2):
        total = in_ref[2 * head, :, QCOLS:].astype(F32) + in_ref[2 * head + 1, :, QCOLS:].astype(F32)
        slim_ref[:, head * HEAD_DIM : (head + 1) * HEAD_DIM] = total.astype(BF)


def unpack(parts):
    per_seq = UNITS // STEP_UNITS
    return pl.pallas_call(
        unpack_body,
        grid=(BATCH, per_seq),
        out_shape=(
            jax.ShapeDtypeStruct((BATCH, LOCAL, D), BF),
            jax.ShapeDtypeStruct((BATCH, LOCAL, KV_HEADS * HEAD_DIM), BF),
        ),
        in_specs=[pl.BlockSpec((STEP_UNITS, LOCAL, PACK), lambda b, i: (b * per_seq + i, 0, 0))],
        out_specs=(
            pl.BlockSpec((None, LOCAL, STEP_UNITS * QCOLS), lambda b, i: (b, 0, i)),
            pl.BlockSpec((None, LOCAL, STEP_UNITS // 2 * HEAD_DIM), lambda b, i: (b, 0, i)),
        ),
        cost_estimate=cost(5),
        compiler_params=PARAMS,
        name="unpack",
    )(parts)


def stack_heads(ref, side):
    rows = pl.ds(pl.multiple_of(side * TOK, TOK), TOK)
    return jnp.concatenate(
        [ref[rows, h * HEAD_DIM : (h + 1) * HEAD_DIM] for h in range(UNIT_HEADS)], axis=0
    )


def fold(chunk, op):
    return op(chunk.reshape(CHUNK // 8, 8, QCOLS), axis=0)


def join(a, b, op):
    return b if a is None else op(a, b)


def chunk_rows(c):
    return slice(c * CHUNK, (c + 1) * CHUNK)


def score_chunk(q, k_ref, s_ref, block, last, top, c):
    s = lax.dot_general(k_ref[chunk_rows(c), :], q, LAST, preferred_element_type=F32)
    if c == last:
        key_pos = c * CHUNK + lax.broadcasted_iota(jnp.int32, (CHUNK, QCOLS), 0)
        query_pos = block * TOK + lax.broadcasted_iota(jnp.int32, (CHUNK, QCOLS), 1) % TOK
        s = jnp.where(key_pos <= query_pos, s, NEG)
    s_ref[c] = s
    return join(top, fold(s, jnp.max), jnp.maximum)


def scaled_grad(g, inverse):
    column = jnp.transpose(jnp.broadcast_to(inverse, (HEAD_DIM, QCOLS)))
    return (g.astype(F32) * column).astype(BF)


def probs_body(q_ref, g_ref, k_ref, low_ref, high_ref, l_ref, dv_ref, s_ref, acc):
    step = pl.program_id(0)

    @pl.when(step == 0)
    def _():
        acc[...] = jnp.zeros_like(acc)

    for last in range(CHUNKS):
        e_ref = low_ref if last < HALF_CHUNKS else high_ref

        @pl.when(step * SIDES // 2 == last)
        def _():
            def one_block(side, carry):
                q = stack_heads(q_ref, side)
                top = None
                for c in range(last + 1):
                    top = score_chunk(q, k_ref, s_ref, step * SIDES + side, last, top, c)
                top = jnp.max(top, axis=0, keepdims=True)
                total = None
                for c in range(last + 1):
                    e = jnp.exp2((s_ref[c] - top) * (SCALE * LOG2E))
                    e_ref[side, c] = e.astype(BF)
                    total = join(total, fold(e, jnp.sum), jnp.add)
                inverse = 1.0 / jnp.sum(total, axis=0, keepdims=True)
                l_ref[side] = inverse
                g = scaled_grad(stack_heads(g_ref, side), inverse)
                for c in range(last + 1):
                    acc[chunk_rows(c), :] += jnp.dot(
                        e_ref[side, c], g, preferred_element_type=F32
                    )
                return carry

            lax.fori_loop(0, SIDES, one_block, 0)

    @pl.when(step == STEPS - 1)
    def _():
        dv_ref[...] = acc[...].astype(BF)


LOW_SPEC = pl.BlockSpec(
    (SIDES, HALF_CHUNKS, CHUNK, QCOLS), lambda t: (jnp.minimum(t, STEPS // 2 - 1), 0, 0, 0)
)
HIGH_SPEC = pl.BlockSpec(
    (SIDES, CHUNKS, CHUNK, QCOLS), lambda t: (jnp.maximum(t - STEPS // 2, 0), 0, 0, 0)
)
STAT_SPEC = pl.BlockSpec((SIDES, 1, QCOLS), lambda t: (t, 0, 0))
Q_SPEC = pl.BlockSpec((SIDES * TOK, QCOLS), lambda t: (t, 0))
G_SPEC = pl.BlockSpec((SIDES * TOK, QCOLS), lambda t: (t, 1))
K_SPEC = pl.BlockSpec((SEQ, HEAD_DIM), lambda t: (0, 2 * UNIT_HEADS))
V_SPEC = pl.BlockSpec((SEQ, HEAD_DIM), lambda t: (0, 2 * UNIT_HEADS + 1))


def attend_probs(packed):
    return pl.pallas_call(
        probs_body,
        grid=(STEPS,),
        out_shape=(
            jax.ShapeDtypeStruct((HALF, HALF_CHUNKS, CHUNK, QCOLS), BF),
            jax.ShapeDtypeStruct((HALF, CHUNKS, CHUNK, QCOLS), BF),
            jax.ShapeDtypeStruct((BLOCKS, 1, QCOLS), F32),
            jax.ShapeDtypeStruct((SEQ, HEAD_DIM), BF),
        ),
        in_specs=[Q_SPEC, G_SPEC, K_SPEC],
        out_specs=(
            LOW_SPEC,
            HIGH_SPEC,
            STAT_SPEC,
            pl.BlockSpec((SEQ, HEAD_DIM), lambda t: (0, 0)),
        ),
        scratch_shapes=[
            pltpu.VMEM((CHUNKS, CHUNK, QCOLS), F32),
            pltpu.VMEM((SEQ, HEAD_DIM), F32),
        ],
        compiler_params=PARAMS,
        cost_estimate=cost(27),
        name="probs",
    )(packed, packed, packed)


def grads_body(
    q_ref, g_ref, k_ref, v_ref, low_ref, high_ref, l_ref, out_ref, p_ref, kt_ref, acc
):
    step = pl.program_id(0)
    place = STEPS - 1 - step

    @pl.when(step == 0)
    def _():
        acc[...] = jnp.zeros_like(acc)
        for c in range(CHUNKS):
            kt_ref[c] = jnp.transpose(k_ref[chunk_rows(c), :])

    for last in range(CHUNKS):
        e_ref = low_ref if last < HALF_CHUNKS else high_ref

        @pl.when(place * SIDES // 2 == last)
        def _():
            def one_block(side, carry):
                inverse = l_ref[side]
                g = scaled_grad(stack_heads(g_ref, side), inverse)
                total = None
                for c in range(last + 1):
                    p = lax.dot_general(
                        v_ref[chunk_rows(c), :], g, LAST, preferred_element_type=F32
                    )
                    p_ref[c] = p
                    total = join(total, fold(p * e_ref[side, c].astype(F32), jnp.sum), jnp.add)
                center = jnp.sum(total, axis=0, keepdims=True) * inverse
                q = stack_heads(q_ref, side)
                dq = None
                for c in range(last + 1):
                    ds = (e_ref[side, c].astype(F32) * (p_ref[c] - center)).astype(BF)
                    acc[chunk_rows(c), :] += jnp.dot(ds, q, preferred_element_type=F32)
                    dq = join(dq, jnp.dot(kt_ref[c], ds, preferred_element_type=F32), jnp.add)
                dq = dq * SCALE
                rows = pl.ds(pl.multiple_of(side * TOK, TOK), TOK)
                for h in range(UNIT_HEADS):
                    cols = slice(h * HEAD_DIM, (h + 1) * HEAD_DIM)
                    out_ref[rows, cols] = jnp.transpose(dq[:, cols]).astype(BF)
                return carry

            lax.fori_loop(0, SIDES, one_block, 0)

    rows = pl.ds(pl.multiple_of(place * SIDES * TOK, SIDES * TOK), SIDES * TOK)
    out_ref[:, QCOLS:] = (acc[rows, :] * SCALE).astype(BF)


def backward(spec):
    index = spec.index_map
    return pl.BlockSpec(spec.block_shape, lambda t: index(STEPS - 1 - t))


def attend_grads(packed, low, high, inverse):
    return pl.pallas_call(
        grads_body,
        grid=(STEPS,),
        out_shape=jax.ShapeDtypeStruct((SEQ, PACK), BF),
        in_specs=[backward(Q_SPEC), backward(G_SPEC), K_SPEC, V_SPEC]
        + [backward(LOW_SPEC), backward(HIGH_SPEC), backward(STAT_SPEC)],
        out_specs=backward(pl.BlockSpec((SIDES * TOK, PACK), lambda t: (t, 0))),
        scratch_shapes=[
            pltpu.VMEM((CHUNKS, CHUNK, QCOLS), F32),
            pltpu.VMEM((CHUNKS, HEAD_DIM, CHUNK), BF),
            pltpu.VMEM((SEQ, HEAD_DIM), F32),
        ],
        compiler_params=PARAMS,
        cost_estimate=cost(27),
        name="grads",
    )(packed, packed, packed, packed, low, high, inverse)


ROWS = BATCH * LOCAL
FEATS = D // DEVICES
PIECES = 8
SECTIONS = 4
HALVES = 2
PART = ROWS // SECTIONS // HALVES


def pair_sums(parts_ref, emit):
    for seq in range(BATCH):
        for head in range(KV_HEADS):
            first = seq * UNITS + 2 * head
            total = parts_ref[first].astype(F32) + parts_ref[first + 1].astype(F32)
            emit(seq, slice(head * HEAD_DIM, (head + 1) * HEAD_DIM), total.astype(BF))


def term_body(here_ref, parts_ref, w_ref, x_ref, gain_ref, top_ref, *refs):
    out_refs, (vg_ref, u_ref, xs_ref, acc) = refs[:-4], refs[-4:]
    step = pl.program_id(0)
    here = here_ref[0]

    @pl.when(step == 0)
    def _():
        acc[...] = jnp.zeros_like(acc)

        def emit(seq, cols, value):
            vg_ref[seq * LOCAL : (seq + 1) * LOCAL, cols] = value

        pair_sums(parts_ref, emit)

    dots = lax.dot_general(vg_ref[...], w_ref[...], LAST, preferred_element_type=F32)
    squares = jnp.zeros((ROWS, 1), F32)
    inner = jnp.zeros((ROWS, 1), F32)
    for i in range(PIECES):
        cols = slice(i * FEATS, (i + 1) * FEATS)
        x = x_ref[:, cols].astype(F32)
        u = dots[:, cols] * gain_ref[:, cols]
        u_ref[step * PIECES + i] = u
        xs_ref[step * PIECES + i] = x_ref[:, cols]
        squares = squares + jnp.sum(x * x, axis=1, keepdims=True)
        inner = inner + jnp.sum(x * u, axis=1, keepdims=True)
    acc[0] += squares
    acc[1] += inner

    @pl.when(step == pl.num_programs(0) - 1)
    def _():
        flag = jnp.where(here == SECTIONS - 1, 1.0, 0.0).astype(F32)
        r = lax.rsqrt(acc[0] * (1.0 / D) + 1e-05)
        acc[1] = acc[1] * (1.0 / D) * (r * r * r)
        acc[0] = r
        for half in range(HALVES * SECTIONS):
            first = ((here + half % SECTIONS) % SECTIONS * HALVES + half // SECTIONS) * PART
            rows = pl.ds(pl.multiple_of(first, PART), PART)
            r = acc[0, rows, :]
            inner = acc[1, rows, :]

            def finish(i, carry):
                cols = pl.ds(pl.multiple_of(i * FEATS, FEATS), FEATS)
                term = r * u_ref[i, rows, :] - xs_ref[i, rows, :].astype(F32) * inner
                term = term + top_ref[rows, cols].astype(F32) * flag
                out_refs[half][:, cols] = term.astype(BF)
                return carry

            lax.fori_loop(0, D // FEATS, finish, 0, unroll=4)


def norm_term(here, parts, weight, x, gain, top):
    width = PIECES * FEATS
    return pl.pallas_call(
        term_body,
        grid=(D // width,),
        out_shape=(jax.ShapeDtypeStruct((PART, D), BF),) * (HALVES * SECTIONS),
        in_specs=[
            pl.BlockSpec(memory_space=pltpu.SMEM),
            pl.BlockSpec((DEVICES, LOCAL, HEAD_DIM), lambda i: (0, 0, 0)),
            pl.BlockSpec((width, KV_HEADS * HEAD_DIM), lambda i: (i, 0)),
            pl.BlockSpec((ROWS, width), lambda i: (0, i)),
            pl.BlockSpec((1, width), lambda i: (0, i)),
            pl.BlockSpec((ROWS, D), lambda i: (0, 0)),
        ],
        out_specs=(pl.BlockSpec((PART, D), lambda i: (0, 0)),) * (HALVES * SECTIONS),
        scratch_shapes=[
            pltpu.VMEM((ROWS, KV_HEADS * HEAD_DIM), BF),
            pltpu.VMEM((D // FEATS, ROWS, FEATS), F32),
            pltpu.VMEM((D // FEATS, ROWS, FEATS), BF),
            pltpu.VMEM((2, ROWS, 1), F32),
        ],
        compiler_params=PARAMS,
        cost_estimate=cost(12),
        name="term",
    )(here, parts, weight, x, gain, top)


def sums_body(here_ref, *refs):
    parts, outs = refs[:SECTIONS], refs[SECTIONS:]
    here = here_ref[0]
    place = [(here - j) % SECTIONS for j in range(SECTIONS)]
    values = [part[...].astype(F32) for part in parts]
    for k in range(SECTIONS):
        total = values[k]
        for j in range(SECTIONS):
            if j != k:
                total = total + values[j] * jnp.where(place[j] > place[k], 1.0, 0.0).astype(F32)
        outs[k][...] = total.astype(BF)


def suffix_sums(here, parts):
    cols = D // 2
    spec = pl.BlockSpec((PART, cols), lambda i: (0, i))
    return pl.pallas_call(
        sums_body,
        grid=(D // cols,),
        out_shape=tuple(jax.ShapeDtypeStruct((PART, D), BF) for _ in range(SECTIONS)),
        in_specs=[pl.BlockSpec(memory_space=pltpu.SMEM)] + [spec] * SECTIONS,
        out_specs=(spec,) * SECTIONS,
        cost_estimate=cost(2),
        compiler_params=PARAMS,
        name="suffix_sums",
    )(here, *parts)


def place_body(here_ref, *refs):
    parts, out_ref = refs[:-1], refs[-1]
    here = here_ref[0]
    for half in range(HALVES * SECTIONS):
        first = ((here + half % SECTIONS) % SECTIONS * HALVES + half // SECTIONS) * PART
        rows = pl.ds(pl.multiple_of(first, PART), PART)
        out_ref[rows, :] = parts[half][...]


def place(here, parts):
    cols = D // 2
    spec = pl.BlockSpec((PART, cols), lambda i: (0, i))
    return pl.pallas_call(
        place_body,
        grid=(D // cols,),
        out_shape=jax.ShapeDtypeStruct((ROWS, D), BF),
        in_specs=[pl.BlockSpec(memory_space=pltpu.SMEM)] + [spec] * (HALVES * SECTIONS),
        out_specs=pl.BlockSpec((ROWS, cols), lambda i: (0, i)),
        cost_estimate=cost(2),
        compiler_params=PARAMS,
        name="place",
    )(here, *parts)


def exchange(parts):
    return lax.all_to_all(parts, "seq", 0, 0, tiled=True)


def turn(array, by):
    pairs = [(i, (i + by) % SECTIONS) for i in range(SECTIONS)]
    return lax.ppermute(array, "section", pairs)


def local(
    layer_input, query_act, key_act, value_act, output_grad, value_weight, norm_gain, top_grad
):
    weight = lax.all_gather(value_weight[0], "seq", axis=0, tiled=True)
    packed = exchange(pack(query_act[0], output_grad[0], key_act[0], value_act[0]))
    packed = packed.reshape(SEQ, 2 * PACK)
    low, high, inverse, dv = attend_probs(packed)
    dv_parts = exchange(dv.reshape(DEVICES, LOCAL, HEAD_DIM))
    grads = attend_grads(packed, low, high, inverse)
    dv_parts, grads = lax.optimization_barrier((dv_parts, grads))
    here = lax.axis_index("section").astype(jnp.int32).reshape(1)
    terms = norm_term(
        here,
        dv_parts,
        weight,
        layer_input[0].reshape(ROWS, D),
        norm_gain,
        top_grad.reshape(ROWS, D),
    )
    grads_back = exchange(grads.reshape(DEVICES, LOCAL, PACK))
    arrived = [
        [terms[half * SECTIONS]] + [turn(terms[half * SECTIONS + k], k) for k in (1, 2, 3)]
        for half in range(HALVES)
    ]
    back = []
    for half in range(HALVES):
        sums = suffix_sums(here, arrived[half])
        back += [sums[0]] + [turn(sums[k], -k) for k in (1, 2, 3)]
    current = place(here, back)
    query_grad, key_grad = unpack(grads_back)
    return current.reshape(1, BATCH, LOCAL, D), query_grad[None], key_grad[None]


def solution(mesh):
    return jax.shard_map(
        local,
        mesh=mesh,
        in_specs=(
            P("section", None, "seq", None),
            P("section", None, "seq", None),
            P("section", None, "seq", None),
            P("section", None, "seq", None),
            P("section", None, "seq", None),
            P("section", "seq", None),
            P("section", None),
            P(None, "seq", None),
        ),
        out_specs=(
            P("section", None, "seq", None),
            P("section", None, "seq", None),
            P("section", None, "seq", None),
        ),
        check_vma=False,
    )
```

```python
import jax
import jax.numpy as jnp
from jax import lax
from jax.experimental import pallas as pl
from jax.experimental.pallas import tpu as pltpu
from jax.sharding import PartitionSpec as P

D = 8192
KV_HEADS = 8
HEAD_DIM = 128
BATCH = 2
SEQ = 2048
DEVICES = 32
LOCAL = SEQ // DEVICES
UNIT_HEADS = 4
QCOLS = UNIT_HEADS * HEAD_DIM
UNITS = DEVICES // BATCH
PACK = QCOLS + HEAD_DIM
STEP_UNITS = 8
TOK = 128
BLOCKS = SEQ // TOK
CHUNK = 256
CHUNKS = SEQ // CHUNK
HALF = BLOCKS // 2
SIDES = 2
STEPS = BLOCKS // SIDES
HALF_CHUNKS = CHUNKS // 2
SCALE = HEAD_DIM ** (-0.5)
LOG2E = 1.4426950408889634
NEG = -1e30

BF = jnp.bfloat16
F32 = jnp.float32
LAST = (((1,), (1,)), ((), ()))


PARAMS = pltpu.CompilerParams(vmem_limit_bytes=60 << 20)


def cost(us):
    return pl.CostEstimate(flops=int(us * 1e9), transcendentals=0, bytes_accessed=0)


def pack_body(q_ref, g_ref, k_ref, v_ref, out_ref):
    for unit in range(STEP_UNITS):
        cols = slice(unit * QCOLS, (unit + 1) * QCOLS)
        kv = slice(unit // 2 * HEAD_DIM, (unit // 2 + 1) * HEAD_DIM)
        out_ref[unit, :, :QCOLS] = q_ref[:, cols]
        out_ref[unit, :, QCOLS : 2 * QCOLS] = g_ref[:, cols]
        out_ref[unit, :, 2 * QCOLS : 2 * QCOLS + HEAD_DIM] = k_ref[:, kv]
        out_ref[unit, :, 2 * QCOLS + HEAD_DIM :] = v_ref[:, kv]


def pack(q, g, k, v):
    wide = pl.BlockSpec((None, LOCAL, STEP_UNITS * QCOLS), lambda b, i: (b, 0, i))
    slim = pl.BlockSpec((None, LOCAL, STEP_UNITS // 2 * HEAD_DIM), lambda b, i: (b, 0, i))
    per_seq = UNITS // STEP_UNITS
    return pl.pallas_call(
        pack_body,
        grid=(BATCH, per_seq),
        out_shape=jax.ShapeDtypeStruct((DEVICES, LOCAL, 2 * PACK), BF),
        in_specs=[wide, wide, slim, slim],
        out_specs=pl.BlockSpec(
            (STEP_UNITS, LOCAL, 2 * PACK), lambda b, i: (b * per_seq + i, 0, 0)
        ),
        compiler_params=PARAMS,
        cost_estimate=cost(6),
        name="pack",
    )(q, g, k, v)


def unpack_body(in_ref, wide_ref, slim_ref):
    for unit in range(STEP_UNITS):
        wide_ref[:, unit * QCOLS : (unit + 1) * QCOLS] = in_ref[unit, :, :QCOLS]
    for head in range(STEP_UNITS // 2):
        total = in_ref[2 * head, :, QCOLS:].astype(F32) + in_ref[2 * head + 1, :, QCOLS:].astype(F32)
        slim_ref[:, head * HEAD_DIM : (head + 1) * HEAD_DIM] = total.astype(BF)


def unpack(parts):
    per_seq = UNITS // STEP_UNITS
    return pl.pallas_call(
        unpack_body,
        grid=(BATCH, per_seq),
        out_shape=(
            jax.ShapeDtypeStruct((BATCH, LOCAL, D), BF),
            jax.ShapeDtypeStruct((BATCH, LOCAL, KV_HEADS * HEAD_DIM), BF),
        ),
        in_specs=[pl.BlockSpec((STEP_UNITS, LOCAL, PACK), lambda b, i: (b * per_seq + i, 0, 0))],
        out_specs=(
            pl.BlockSpec((None, LOCAL, STEP_UNITS * QCOLS), lambda b, i: (b, 0, i)),
            pl.BlockSpec((None, LOCAL, STEP_UNITS // 2 * HEAD_DIM), lambda b, i: (b, 0, i)),
        ),
        cost_estimate=cost(5),
        compiler_params=PARAMS,
        name="unpack",
    )(parts)


def stack_heads(ref, side):
    rows = pl.ds(pl.multiple_of(side * TOK, TOK), TOK)
    return jnp.concatenate(
        [ref[rows, h * HEAD_DIM : (h + 1) * HEAD_DIM] for h in range(UNIT_HEADS)], axis=0
    )


def fold(chunk, op):
    return op(chunk.reshape(CHUNK // 8, 8, QCOLS), axis=0)


def join(a, b, op):
    return b if a is None else op(a, b)


def chunk_rows(c):
    return slice(c * CHUNK, (c + 1) * CHUNK)


def score_chunk(q, k_ref, s_ref, block, last, top, c):
    s = lax.dot_general(k_ref[chunk_rows(c), :], q, LAST, preferred_element_type=F32)
    if c == last:
        key_pos = c * CHUNK + lax.broadcasted_iota(jnp.int32, (CHUNK, QCOLS), 0)
        query_pos = block * TOK + lax.broadcasted_iota(jnp.int32, (CHUNK, QCOLS), 1) % TOK
        s = jnp.where(key_pos <= query_pos, s, NEG)
    s_ref[c] = s
    return join(top, fold(s, jnp.max), jnp.maximum)


def scaled_grad(g, inverse):
    column = jnp.transpose(jnp.broadcast_to(inverse, (HEAD_DIM, QCOLS)))
    return (g.astype(F32) * column).astype(BF)


def probs_body(q_ref, g_ref, k_ref, low_ref, high_ref, l_ref, dv_ref, s_ref, acc):
    step = pl.program_id(0)

    @pl.when(step == 0)
    def _():
        acc[...] = jnp.zeros_like(acc)

    for last in range(CHUNKS):
        e_ref = low_ref if last < HALF_CHUNKS else high_ref

        @pl.when(step * SIDES // 2 == last)
        def _():
            def one_block(side, carry):
                q = stack_heads(q_ref, side)
                top = None
                for c in range(last + 1):
                    top = score_chunk(q, k_ref, s_ref, step * SIDES + side, last, top, c)
                top = jnp.max(top, axis=0, keepdims=True)
                total = None
                for c in range(last + 1):
                    e = jnp.exp2((s_ref[c] - top) * (SCALE * LOG2E))
                    e_ref[side, c] = e.astype(BF)
                    total = join(total, fold(e, jnp.sum), jnp.add)
                inverse = 1.0 / jnp.sum(total, axis=0, keepdims=True)
                l_ref[side] = inverse
                g = scaled_grad(stack_heads(g_ref, side), inverse)
                for c in range(last + 1):
                    acc[chunk_rows(c), :] += jnp.dot(
                        e_ref[side, c], g, preferred_element_type=F32
                    )
                return carry

            lax.fori_loop(0, SIDES, one_block, 0)

    @pl.when(step == STEPS - 1)
    def _():
        dv_ref[...] = acc[...].astype(BF)


LOW_SPEC = pl.BlockSpec(
    (SIDES, HALF_CHUNKS, CHUNK, QCOLS), lambda t: (jnp.minimum(t, STEPS // 2 - 1), 0, 0, 0)
)
HIGH_SPEC = pl.BlockSpec(
    (SIDES, CHUNKS, CHUNK, QCOLS), lambda t: (jnp.maximum(t - STEPS // 2, 0), 0, 0, 0)
)
STAT_SPEC = pl.BlockSpec((SIDES, 1, QCOLS), lambda t: (t, 0, 0))
Q_SPEC = pl.BlockSpec((SIDES * TOK, QCOLS), lambda t: (t, 0))
G_SPEC = pl.BlockSpec((SIDES * TOK, QCOLS), lambda t: (t, 1))
K_SPEC = pl.BlockSpec((SEQ, HEAD_DIM), lambda t: (0, 2 * UNIT_HEADS))
V_SPEC = pl.BlockSpec((SEQ, HEAD_DIM), lambda t: (0, 2 * UNIT_HEADS + 1))


def attend_probs(packed):
    return pl.pallas_call(
        probs_body,
        grid=(STEPS,),
        out_shape=(
            jax.ShapeDtypeStruct((HALF, HALF_CHUNKS, CHUNK, QCOLS), BF),
            jax.ShapeDtypeStruct((HALF, CHUNKS, CHUNK, QCOLS), BF),
            jax.ShapeDtypeStruct((BLOCKS, 1, QCOLS), F32),
            jax.ShapeDtypeStruct((SEQ, HEAD_DIM), BF),
        ),
        in_specs=[Q_SPEC, G_SPEC, K_SPEC],
        out_specs=(
            LOW_SPEC,
            HIGH_SPEC,
            STAT_SPEC,
            pl.BlockSpec((SEQ, HEAD_DIM), lambda t: (0, 0)),
        ),
        scratch_shapes=[
            pltpu.VMEM((CHUNKS, CHUNK, QCOLS), F32),
            pltpu.VMEM((SEQ, HEAD_DIM), F32),
        ],
        compiler_params=PARAMS,
        cost_estimate=cost(27),
        name="probs",
    )(packed, packed, packed)


def grads_body(
    q_ref, g_ref, k_ref, v_ref, low_ref, high_ref, l_ref, out_ref, p_ref, kt_ref, acc
):
    step = pl.program_id(0)
    place = STEPS - 1 - step

    @pl.when(step == 0)
    def _():
        acc[...] = jnp.zeros_like(acc)
        for c in range(CHUNKS):
            kt_ref[c] = jnp.transpose(k_ref[chunk_rows(c), :])

    for last in range(CHUNKS):
        e_ref = low_ref if last < HALF_CHUNKS else high_ref

        @pl.when(place * SIDES // 2 == last)
        def _():
            def one_block(side, carry):
                inverse = l_ref[side]
                g = scaled_grad(stack_heads(g_ref, side), inverse)
                total = None
                for c in range(last + 1):
                    p = lax.dot_general(
                        v_ref[chunk_rows(c), :], g, LAST, preferred_element_type=F32
                    )
                    p_ref[c] = p
                    total = join(total, fold(p * e_ref[side, c].astype(F32), jnp.sum), jnp.add)
                center = jnp.sum(total, axis=0, keepdims=True) * inverse
                q = stack_heads(q_ref, side)
                dq = None
                for c in range(last + 1):
                    ds = (e_ref[side, c].astype(F32) * (p_ref[c] - center)).astype(BF)
                    acc[chunk_rows(c), :] += jnp.dot(ds, q, preferred_element_type=F32)
                    dq = join(dq, jnp.dot(kt_ref[c], ds, preferred_element_type=F32), jnp.add)
                dq = dq * SCALE
                rows = pl.ds(pl.multiple_of(side * TOK, TOK), TOK)
                for h in range(UNIT_HEADS):
                    cols = slice(h * HEAD_DIM, (h + 1) * HEAD_DIM)
                    out_ref[rows, cols] = jnp.transpose(dq[:, cols]).astype(BF)
                return carry

            lax.fori_loop(0, SIDES, one_block, 0)

    rows = pl.ds(pl.multiple_of(place * SIDES * TOK, SIDES * TOK), SIDES * TOK)
    out_ref[:, QCOLS:] = (acc[rows, :] * SCALE).astype(BF)


def backward(spec):
    index = spec.index_map
    return pl.BlockSpec(spec.block_shape, lambda t: index(STEPS - 1 - t))


def attend_grads(packed, low, high, inverse):
    return pl.pallas_call(
        grads_body,
        grid=(STEPS,),
        out_shape=jax.ShapeDtypeStruct((SEQ, PACK), BF),
        in_specs=[backward(Q_SPEC), backward(G_SPEC), K_SPEC, V_SPEC]
        + [backward(LOW_SPEC), backward(HIGH_SPEC), backward(STAT_SPEC)],
        out_specs=backward(pl.BlockSpec((SIDES * TOK, PACK), lambda t: (t, 0))),
        scratch_shapes=[
            pltpu.VMEM((CHUNKS, CHUNK, QCOLS), F32),
            pltpu.VMEM((CHUNKS, HEAD_DIM, CHUNK), BF),
            pltpu.VMEM((SEQ, HEAD_DIM), F32),
        ],
        compiler_params=PARAMS,
        cost_estimate=cost(27),
        name="grads",
    )(packed, packed, packed, packed, low, high, inverse)


ROWS = BATCH * LOCAL
FEATS = D // DEVICES
PIECES = 8
SECTIONS = 4
HALVES = 2
PART = ROWS // SECTIONS // HALVES


def pair_sums(parts_ref, emit):
    for seq in range(BATCH):
        for head in range(KV_HEADS):
            first = seq * UNITS + 2 * head
            total = parts_ref[first].astype(F32) + parts_ref[first + 1].astype(F32)
            emit(seq, slice(head * HEAD_DIM, (head + 1) * HEAD_DIM), total.astype(BF))


def halves_sum(piece):
    return piece[:, :HEAD_DIM] + piece[:, HEAD_DIM:]


def term_body(here_ref, parts_ref, w_ref, x_ref, gain_ref, top_ref, *refs):
    out_refs, (vg_ref, u_ref, xs_ref, acc) = refs[:-4], refs[-4:]
    step = pl.program_id(0)
    here = here_ref[0]

    @pl.when(step == 0)
    def _():
        acc[...] = jnp.zeros_like(acc)

        def emit(seq, cols, value):
            vg_ref[seq * LOCAL : (seq + 1) * LOCAL, cols] = value

        pair_sums(parts_ref, emit)

    dots = lax.dot_general(vg_ref[...], w_ref[...], LAST, preferred_element_type=F32)
    squares = acc[0]
    inner = acc[1]
    for i in range(PIECES):
        cols = slice(i * FEATS, (i + 1) * FEATS)
        x = x_ref[:, cols].astype(F32)
        u = dots[:, cols] * gain_ref[:, cols]
        u_ref[step * PIECES + i] = u
        xs_ref[step * PIECES + i] = x_ref[:, cols]
        squares = squares + halves_sum(x * x)
        inner = inner + halves_sum(x * u)
    acc[0] = squares
    acc[1] = inner

    @pl.when(step == pl.num_programs(0) - 1)
    def _():
        flag = jnp.where(here == SECTIONS - 1, 1.0, 0.0).astype(F32)
        r = lax.rsqrt(jnp.sum(acc[0], axis=1, keepdims=True) * (1.0 / D) + 1e-05)
        inner = jnp.sum(acc[1], axis=1, keepdims=True) * (1.0 / D) * (r * r * r)
        acc[0] = jnp.broadcast_to(r, (ROWS, HEAD_DIM))
        acc[1] = jnp.broadcast_to(inner, (ROWS, HEAD_DIM))
        for half in range(HALVES * SECTIONS):
            first = ((here + half % SECTIONS) % SECTIONS * HALVES + half // SECTIONS) * PART
            rows = pl.ds(pl.multiple_of(first, PART), PART)
            r = jnp.concatenate([acc[0, rows, :]] * (FEATS // HEAD_DIM), axis=1)
            inner = jnp.concatenate([acc[1, rows, :]] * (FEATS // HEAD_DIM), axis=1)

            def finish(i, carry):
                cols = pl.ds(pl.multiple_of(i * FEATS, FEATS), FEATS)
                term = r * u_ref[i, rows, :] - xs_ref[i, rows, :].astype(F32) * inner
                term = term + top_ref[rows, cols].astype(F32) * flag
                out_refs[half][:, cols] = term.astype(BF)
                return carry

            lax.fori_loop(0, D // FEATS, finish, 0, unroll=16)


def norm_term(here, parts, weight, x, gain, top):
    width = PIECES * FEATS
    return pl.pallas_call(
        term_body,
        grid=(D // width,),
        out_shape=(jax.ShapeDtypeStruct((PART, D), BF),) * (HALVES * SECTIONS),
        in_specs=[
            pl.BlockSpec(memory_space=pltpu.SMEM),
            pl.BlockSpec((DEVICES, LOCAL, HEAD_DIM), lambda i: (0, 0, 0)),
            pl.BlockSpec((width, KV_HEADS * HEAD_DIM), lambda i: (i, 0)),
            pl.BlockSpec((ROWS, width), lambda i: (0, i)),
            pl.BlockSpec((1, width), lambda i: (0, i)),
            pl.BlockSpec((ROWS, D), lambda i: (0, 0)),
        ],
        out_specs=(pl.BlockSpec((PART, D), lambda i: (0, 0)),) * (HALVES * SECTIONS),
        scratch_shapes=[
            pltpu.VMEM((ROWS, KV_HEADS * HEAD_DIM), BF),
            pltpu.VMEM((D // FEATS, ROWS, FEATS), F32),
            pltpu.VMEM((D // FEATS, ROWS, FEATS), BF),
            pltpu.VMEM((2, ROWS, HEAD_DIM), F32),
        ],
        compiler_params=PARAMS,
        cost_estimate=cost(12),
        name="term",
    )(here, parts, weight, x, gain, top)


def sums_body(here_ref, *refs):
    parts, outs = refs[:SECTIONS], refs[SECTIONS:]
    here = here_ref[0]
    place = [(here - j) % SECTIONS for j in range(SECTIONS)]
    values = [part[...].astype(F32) for part in parts]
    for k in range(SECTIONS):
        total = values[k]
        for j in range(SECTIONS):
            if j != k:
                total = total + values[j] * jnp.where(place[j] > place[k], 1.0, 0.0).astype(F32)
        outs[k][...] = total.astype(BF)


def suffix_sums(here, parts):
    cols = D // 2
    spec = pl.BlockSpec((PART, cols), lambda i: (0, i))
    return pl.pallas_call(
        sums_body,
        grid=(D // cols,),
        out_shape=tuple(jax.ShapeDtypeStruct((PART, D), BF) for _ in range(SECTIONS)),
        in_specs=[pl.BlockSpec(memory_space=pltpu.SMEM)] + [spec] * SECTIONS,
        out_specs=(spec,) * SECTIONS,
        cost_estimate=cost(2),
        compiler_params=PARAMS,
        name="suffix_sums",
    )(here, *parts)


def place_body(here_ref, *refs):
    parts, out_ref = refs[:-1], refs[-1]
    here = here_ref[0]
    for half in range(HALVES * SECTIONS):
        first = ((here + half % SECTIONS) % SECTIONS * HALVES + half // SECTIONS) * PART
        rows = pl.ds(pl.multiple_of(first, PART), PART)
        out_ref[rows, :] = parts[half][...]


def place(here, parts):
    cols = D // 2
    spec = pl.BlockSpec((PART, cols), lambda i: (0, i))
    return pl.pallas_call(
        place_body,
        grid=(D // cols,),
        out_shape=jax.ShapeDtypeStruct((ROWS, D), BF),
        in_specs=[pl.BlockSpec(memory_space=pltpu.SMEM)] + [spec] * (HALVES * SECTIONS),
        out_specs=pl.BlockSpec((ROWS, cols), lambda i: (0, i)),
        cost_estimate=cost(2),
        compiler_params=PARAMS,
        name="place",
    )(here, *parts)


def exchange(parts):
    return lax.all_to_all(parts, "seq", 0, 0, tiled=True)


def turn(array, by):
    pairs = [(i, (i + by) % SECTIONS) for i in range(SECTIONS)]
    return lax.ppermute(array, "section", pairs)


def local(
    layer_input, query_act, key_act, value_act, output_grad, value_weight, norm_gain, top_grad
):
    weight = lax.all_gather(value_weight[0], "seq", axis=0, tiled=True)
    packed = exchange(pack(query_act[0], output_grad[0], key_act[0], value_act[0]))
    packed = packed.reshape(SEQ, 2 * PACK)
    low, high, inverse, dv = attend_probs(packed)
    dv_parts = exchange(dv.reshape(DEVICES, LOCAL, HEAD_DIM))
    grads = attend_grads(packed, low, high, inverse)
    dv_parts, grads = lax.optimization_barrier((dv_parts, grads))
    here = lax.axis_index("section").astype(jnp.int32).reshape(1)
    terms = norm_term(
        here,
        dv_parts,
        weight,
        layer_input[0].reshape(ROWS, D),
        norm_gain,
        top_grad.reshape(ROWS, D),
    )
    grads_back = exchange(grads.reshape(DEVICES, LOCAL, PACK))
    arrived = [
        [terms[half * SECTIONS]] + [turn(terms[half * SECTIONS + k], k) for k in (1, 2, 3)]
        for half in range(HALVES)
    ]
    back = []
    for half in range(HALVES):
        sums = suffix_sums(here, arrived[half])
        back += [sums[0]] + [turn(sums[k], -k) for k in (1, 2, 3)]
    current = place(here, back)
    query_grad, key_grad = unpack(grads_back)
    return current.reshape(1, BATCH, LOCAL, D), query_grad[None], key_grad[None]


def solution(mesh):
    return jax.shard_map(
        local,
        mesh=mesh,
        in_specs=(
            P("section", None, "seq", None),
            P("section", None, "seq", None),
            P("section", None, "seq", None),
            P("section", None, "seq", None),
            P("section", None, "seq", None),
            P("section", "seq", None),
            P("section", None),
            P(None, "seq", None),
        ),
        out_specs=(
            P("section", None, "seq", None),
            P("section", None, "seq", None),
            P("section", None, "seq", None),
        ),
        check_vma=False,
    )
```

```python
import jax
import jax.numpy as jnp
from jax import lax
from jax.experimental import pallas as pl
from jax.experimental.pallas import tpu as pltpu
from jax.sharding import PartitionSpec as P

D = 8192
KV_HEADS = 8
HEAD_DIM = 128
BATCH = 2
SEQ = 2048
DEVICES = 32
LOCAL = SEQ // DEVICES
UNIT_HEADS = 4
QCOLS = UNIT_HEADS * HEAD_DIM
UNITS = DEVICES // BATCH
PACK = QCOLS + HEAD_DIM
STEP_UNITS = 8
TOK = 128
BLOCKS = SEQ // TOK
CHUNK = 256
CHUNKS = SEQ // CHUNK
HALF = BLOCKS // 2
SIDES = 2
STEPS = BLOCKS // SIDES
HALF_CHUNKS = CHUNKS // 2
SCALE = HEAD_DIM ** (-0.5)
LOG2E = 1.4426950408889634
NEG = -1e30

BF = jnp.bfloat16
F32 = jnp.float32
LAST = (((1,), (1,)), ((), ()))


PARAMS = pltpu.CompilerParams(vmem_limit_bytes=60 << 20)
SMALL = pltpu.CompilerParams(vmem_limit_bytes=32 << 20)


def cost(us):
    return pl.CostEstimate(flops=int(us * 1e9), transcendentals=0, bytes_accessed=0)


def pack_body(q_ref, g_ref, k_ref, v_ref, out_ref):
    for unit in range(STEP_UNITS):
        cols = slice(unit * QCOLS, (unit + 1) * QCOLS)
        kv = slice(unit // 2 * HEAD_DIM, (unit // 2 + 1) * HEAD_DIM)
        out_ref[unit, :, :QCOLS] = q_ref[:, cols]
        out_ref[unit, :, QCOLS : 2 * QCOLS] = g_ref[:, cols]
        out_ref[unit, :, 2 * QCOLS : 2 * QCOLS + HEAD_DIM] = k_ref[:, kv]
        out_ref[unit, :, 2 * QCOLS + HEAD_DIM :] = v_ref[:, kv]


def pack(q, g, k, v):
    wide = pl.BlockSpec((None, LOCAL, STEP_UNITS * QCOLS), lambda b, i: (b, 0, i))
    slim = pl.BlockSpec((None, LOCAL, STEP_UNITS // 2 * HEAD_DIM), lambda b, i: (b, 0, i))
    per_seq = UNITS // STEP_UNITS
    return pl.pallas_call(
        pack_body,
        grid=(BATCH, per_seq),
        out_shape=jax.ShapeDtypeStruct((DEVICES, LOCAL, 2 * PACK), BF),
        in_specs=[wide, wide, slim, slim],
        out_specs=pl.BlockSpec(
            (STEP_UNITS, LOCAL, 2 * PACK), lambda b, i: (b * per_seq + i, 0, 0)
        ),
        compiler_params=PARAMS,
        cost_estimate=cost(6),
        name="pack",
    )(q, g, k, v)


def unpack_body(in_ref, wide_ref, slim_ref):
    for unit in range(STEP_UNITS):
        wide_ref[:, unit * QCOLS : (unit + 1) * QCOLS] = in_ref[unit, :, :QCOLS]
    for head in range(STEP_UNITS // 2):
        total = in_ref[2 * head, :, QCOLS:].astype(F32) + in_ref[2 * head + 1, :, QCOLS:].astype(F32)
        slim_ref[:, head * HEAD_DIM : (head + 1) * HEAD_DIM] = total.astype(BF)


def unpack(parts):
    per_seq = UNITS // STEP_UNITS
    return pl.pallas_call(
        unpack_body,
        grid=(BATCH, per_seq),
        out_shape=(
            jax.ShapeDtypeStruct((BATCH, LOCAL, D), BF),
            jax.ShapeDtypeStruct((BATCH, LOCAL, KV_HEADS * HEAD_DIM), BF),
        ),
        in_specs=[pl.BlockSpec((STEP_UNITS, LOCAL, PACK), lambda b, i: (b * per_seq + i, 0, 0))],
        out_specs=(
            pl.BlockSpec((None, LOCAL, STEP_UNITS * QCOLS), lambda b, i: (b, 0, i)),
            pl.BlockSpec((None, LOCAL, STEP_UNITS // 2 * HEAD_DIM), lambda b, i: (b, 0, i)),
        ),
        cost_estimate=cost(5),
        compiler_params=SMALL,
        name="unpack",
    )(parts)


def stack_heads(ref, side):
    rows = pl.ds(pl.multiple_of(side * TOK, TOK), TOK)
    return jnp.concatenate(
        [ref[rows, h * HEAD_DIM : (h + 1) * HEAD_DIM] for h in range(UNIT_HEADS)], axis=0
    )


def fold(chunk, op):
    return op(chunk.reshape(CHUNK // 8, 8, QCOLS), axis=0)


def join(a, b, op):
    return b if a is None else op(a, b)


def chunk_rows(c):
    return slice(c * CHUNK, (c + 1) * CHUNK)


def score_chunk(q, k_ref, s_ref, block, last, top, c):
    s = lax.dot_general(k_ref[chunk_rows(c), :], q, LAST, preferred_element_type=F32)
    if c == last:
        key_pos = c * CHUNK + lax.broadcasted_iota(jnp.int32, (CHUNK, QCOLS), 0)
        query_pos = block * TOK + lax.broadcasted_iota(jnp.int32, (CHUNK, QCOLS), 1) % TOK
        s = jnp.where(key_pos <= query_pos, s, NEG)
    s_ref[c] = s
    return join(top, fold(s, jnp.max), jnp.maximum)


def scaled_grad(g, inverse):
    column = jnp.transpose(jnp.broadcast_to(inverse, (HEAD_DIM, QCOLS)))
    return (g.astype(F32) * column).astype(BF)


def probs_body(q_ref, g_ref, k_ref, low_ref, high_ref, l_ref, dv_ref, s_ref, acc):
    step = pl.program_id(0)

    @pl.when(step == 0)
    def _():
        acc[...] = jnp.zeros_like(acc)

    for last in range(CHUNKS):
        e_ref = low_ref if last < HALF_CHUNKS else high_ref

        @pl.when(step * SIDES // 2 == last)
        def _():
            def one_block(side, carry):
                q = stack_heads(q_ref, side)
                top = None
                for c in range(last + 1):
                    top = score_chunk(q, k_ref, s_ref, step * SIDES + side, last, top, c)
                top = jnp.max(top, axis=0, keepdims=True)
                total = None
                for c in range(last + 1):
                    e = jnp.exp2((s_ref[c] - top) * (SCALE * LOG2E))
                    e_ref[side, c] = e.astype(BF)
                    total = join(total, fold(e, jnp.sum), jnp.add)
                inverse = 1.0 / jnp.sum(total, axis=0, keepdims=True)
                l_ref[side] = inverse
                g = scaled_grad(stack_heads(g_ref, side), inverse)
                for c in range(last + 1):
                    acc[chunk_rows(c), :] += jnp.dot(
                        e_ref[side, c], g, preferred_element_type=F32
                    )
                return carry

            lax.fori_loop(0, SIDES, one_block, 0)

    @pl.when(step == STEPS - 1)
    def _():
        dv_ref[...] = acc[...].astype(BF)


LOW_SPEC = pl.BlockSpec(
    (SIDES, HALF_CHUNKS, CHUNK, QCOLS), lambda t: (jnp.minimum(t, STEPS // 2 - 1), 0, 0, 0)
)
HIGH_SPEC = pl.BlockSpec(
    (SIDES, CHUNKS, CHUNK, QCOLS), lambda t: (jnp.maximum(t - STEPS // 2, 0), 0, 0, 0)
)
STAT_SPEC = pl.BlockSpec((SIDES, 1, QCOLS), lambda t: (t, 0, 0))
Q_SPEC = pl.BlockSpec((SIDES * TOK, QCOLS), lambda t: (t, 0))
G_SPEC = pl.BlockSpec((SIDES * TOK, QCOLS), lambda t: (t, 1))
K_SPEC = pl.BlockSpec((SEQ, HEAD_DIM), lambda t: (0, 2 * UNIT_HEADS))
V_SPEC = pl.BlockSpec((SEQ, HEAD_DIM), lambda t: (0, 2 * UNIT_HEADS + 1))


def attend_probs(packed):
    return pl.pallas_call(
        probs_body,
        grid=(STEPS,),
        out_shape=(
            jax.ShapeDtypeStruct((HALF, HALF_CHUNKS, CHUNK, QCOLS), BF),
            jax.ShapeDtypeStruct((HALF, CHUNKS, CHUNK, QCOLS), BF),
            jax.ShapeDtypeStruct((BLOCKS, 1, QCOLS), F32),
            jax.ShapeDtypeStruct((SEQ, HEAD_DIM), BF),
        ),
        in_specs=[Q_SPEC, G_SPEC, K_SPEC],
        out_specs=(
            LOW_SPEC,
            HIGH_SPEC,
            STAT_SPEC,
            pl.BlockSpec((SEQ, HEAD_DIM), lambda t: (0, 0)),
        ),
        scratch_shapes=[
            pltpu.VMEM((CHUNKS, CHUNK, QCOLS), F32),
            pltpu.VMEM((SEQ, HEAD_DIM), F32),
        ],
        compiler_params=PARAMS,
        cost_estimate=cost(27),
        name="probs",
    )(packed, packed, packed)


def grads_body(
    q_ref, g_ref, k_ref, v_ref, low_ref, high_ref, l_ref, out_ref, p_ref, kt_ref, acc
):
    step = pl.program_id(0)
    place = STEPS - 1 - step

    @pl.when(step == 0)
    def _():
        acc[...] = jnp.zeros_like(acc)
        for c in range(CHUNKS):
            kt_ref[c] = jnp.transpose(k_ref[chunk_rows(c), :])

    for last in range(CHUNKS):
        e_ref = low_ref if last < HALF_CHUNKS else high_ref

        @pl.when(place * SIDES // 2 == last)
        def _():
            def one_block(side, carry):
                inverse = l_ref[side]
                g = scaled_grad(stack_heads(g_ref, side), inverse)
                total = None
                for c in range(last + 1):
                    p = lax.dot_general(
                        v_ref[chunk_rows(c), :], g, LAST, preferred_element_type=F32
                    )
                    p_ref[c] = p
                    total = join(total, fold(p * e_ref[side, c].astype(F32), jnp.sum), jnp.add)
                center = jnp.sum(total, axis=0, keepdims=True) * inverse
                q = stack_heads(q_ref, side)
                dq = None
                for c in range(last + 1):
                    ds = (e_ref[side, c].astype(F32) * (p_ref[c] - center)).astype(BF)
                    acc[chunk_rows(c), :] += jnp.dot(ds, q, preferred_element_type=F32)
                    dq = join(dq, jnp.dot(kt_ref[c], ds, preferred_element_type=F32), jnp.add)
                dq = dq * SCALE
                rows = pl.ds(pl.multiple_of(side * TOK, TOK), TOK)
                for h in range(UNIT_HEADS):
                    cols = slice(h * HEAD_DIM, (h + 1) * HEAD_DIM)
                    out_ref[rows, cols] = jnp.transpose(dq[:, cols]).astype(BF)
                return carry

            lax.fori_loop(0, SIDES, one_block, 0)

    rows = pl.ds(pl.multiple_of(place * SIDES * TOK, SIDES * TOK), SIDES * TOK)
    out_ref[:, QCOLS:] = (acc[rows, :] * SCALE).astype(BF)


def backward(spec):
    index = spec.index_map
    return pl.BlockSpec(spec.block_shape, lambda t: index(STEPS - 1 - t))


def attend_grads(packed, low, high, inverse):
    return pl.pallas_call(
        grads_body,
        grid=(STEPS,),
        out_shape=jax.ShapeDtypeStruct((SEQ, PACK), BF),
        in_specs=[backward(Q_SPEC), backward(G_SPEC), K_SPEC, V_SPEC]
        + [backward(LOW_SPEC), backward(HIGH_SPEC), backward(STAT_SPEC)],
        out_specs=backward(pl.BlockSpec((SIDES * TOK, PACK), lambda t: (t, 0))),
        scratch_shapes=[
            pltpu.VMEM((CHUNKS, CHUNK, QCOLS), F32),
            pltpu.VMEM((CHUNKS, HEAD_DIM, CHUNK), BF),
            pltpu.VMEM((SEQ, HEAD_DIM), F32),
        ],
        compiler_params=PARAMS,
        cost_estimate=cost(27),
        name="grads",
    )(packed, packed, packed, packed, low, high, inverse)


ROWS = BATCH * LOCAL
FEATS = D // DEVICES
PIECES = 8
SECTIONS = 4
HALVES = 2
PART = ROWS // SECTIONS // HALVES


def pair_sums(parts_ref, emit):
    for seq in range(BATCH):
        for head in range(KV_HEADS):
            first = seq * UNITS + 2 * head
            total = parts_ref[first].astype(F32) + parts_ref[first + 1].astype(F32)
            emit(seq, slice(head * HEAD_DIM, (head + 1) * HEAD_DIM), total.astype(BF))


def halves_sum(piece):
    return piece[:, :HEAD_DIM] + piece[:, HEAD_DIM:]


def term_body(here_ref, parts_ref, w_ref, x_ref, gain_ref, top_ref, *refs):
    out_refs, (vg_ref, u_ref, xs_ref, acc) = refs[:-4], refs[-4:]
    step = pl.program_id(0)
    here = here_ref[0]

    @pl.when(step == 0)
    def _():
        acc[...] = jnp.zeros_like(acc)

        def emit(seq, cols, value):
            vg_ref[seq * LOCAL : (seq + 1) * LOCAL, cols] = value

        pair_sums(parts_ref, emit)

    dots = lax.dot_general(vg_ref[...], w_ref[...], LAST, preferred_element_type=F32)
    squares = acc[0]
    inner = acc[1]
    for i in range(PIECES):
        cols = slice(i * FEATS, (i + 1) * FEATS)
        x = x_ref[:, cols].astype(F32)
        u = dots[:, cols] * gain_ref[:, cols]
        u_ref[step * PIECES + i] = u
        xs_ref[step * PIECES + i] = x_ref[:, cols]
        squares = squares + halves_sum(x * x)
        inner = inner + halves_sum(x * u)
    acc[0] = squares
    acc[1] = inner

    @pl.when(step == pl.num_programs(0) - 1)
    def _():
        flag = jnp.where(here == SECTIONS - 1, 1.0, 0.0).astype(F32)
        r = lax.rsqrt(jnp.sum(acc[0], axis=1, keepdims=True) * (1.0 / D) + 1e-05)
        inner = jnp.sum(acc[1], axis=1, keepdims=True) * (1.0 / D) * (r * r * r)
        acc[0] = jnp.broadcast_to(r, (ROWS, HEAD_DIM))
        acc[1] = jnp.broadcast_to(inner, (ROWS, HEAD_DIM))
        for half in range(HALVES * SECTIONS):
            first = ((here + half % SECTIONS) % SECTIONS * HALVES + half // SECTIONS) * PART
            rows = pl.ds(pl.multiple_of(first, PART), PART)
            r = jnp.concatenate([acc[0, rows, :]] * (FEATS // HEAD_DIM), axis=1)
            inner = jnp.concatenate([acc[1, rows, :]] * (FEATS // HEAD_DIM), axis=1)

            def finish(i, carry):
                cols = pl.ds(pl.multiple_of(i * FEATS, FEATS), FEATS)
                term = r * u_ref[i, rows, :] - xs_ref[i, rows, :].astype(F32) * inner
                term = term + top_ref[rows, cols].astype(F32) * flag
                out_refs[half][:, cols] = term.astype(BF)
                return carry

            lax.fori_loop(0, D // FEATS, finish, 0, unroll=16)


def norm_term(here, parts, weight, x, gain, top):
    width = PIECES * FEATS
    return pl.pallas_call(
        term_body,
        grid=(D // width,),
        out_shape=(jax.ShapeDtypeStruct((PART, D), BF),) * (HALVES * SECTIONS),
        in_specs=[
            pl.BlockSpec(memory_space=pltpu.SMEM),
            pl.BlockSpec((DEVICES, LOCAL, HEAD_DIM), lambda i: (0, 0, 0)),
            pl.BlockSpec((width, KV_HEADS * HEAD_DIM), lambda i: (i, 0)),
            pl.BlockSpec((ROWS, width), lambda i: (0, i)),
            pl.BlockSpec((1, width), lambda i: (0, i)),
            pl.BlockSpec((ROWS, D), lambda i: (0, 0)),
        ],
        out_specs=(pl.BlockSpec((PART, D), lambda i: (0, 0)),) * (HALVES * SECTIONS),
        scratch_shapes=[
            pltpu.VMEM((ROWS, KV_HEADS * HEAD_DIM), BF),
            pltpu.VMEM((D // FEATS, ROWS, FEATS), F32),
            pltpu.VMEM((D // FEATS, ROWS, FEATS), BF),
            pltpu.VMEM((2, ROWS, HEAD_DIM), F32),
        ],
        compiler_params=PARAMS,
        cost_estimate=cost(12),
        name="term",
    )(here, parts, weight, x, gain, top)


def sums_body(here_ref, *refs):
    parts, outs = refs[:SECTIONS], refs[SECTIONS:]
    here = here_ref[0]
    place = [(here - j) % SECTIONS for j in range(SECTIONS)]
    values = [part[...].astype(F32) for part in parts]
    for k in range(SECTIONS):
        total = values[k]
        for j in range(SECTIONS):
            if j != k:
                total = total + values[j] * jnp.where(place[j] > place[k], 1.0, 0.0).astype(F32)
        outs[k][...] = total.astype(BF)


def suffix_sums(here, parts):
    cols = D // 2
    spec = pl.BlockSpec((PART, cols), lambda i: (0, i))
    return pl.pallas_call(
        sums_body,
        grid=(D // cols,),
        out_shape=tuple(jax.ShapeDtypeStruct((PART, D), BF) for _ in range(SECTIONS)),
        in_specs=[pl.BlockSpec(memory_space=pltpu.SMEM)] + [spec] * SECTIONS,
        out_specs=(spec,) * SECTIONS,
        cost_estimate=cost(2),
        compiler_params=SMALL,
        name="suffix_sums",
    )(here, *parts)


def place_body(here_ref, *refs):
    parts, out_ref = refs[:-1], refs[-1]
    here = here_ref[0]
    for half in range(HALVES * SECTIONS):
        first = ((here + half % SECTIONS) % SECTIONS * HALVES + half // SECTIONS) * PART
        rows = pl.ds(pl.multiple_of(first, PART), PART)
        out_ref[rows, :] = parts[half][...]


def place(here, parts):
    cols = D // 2
    spec = pl.BlockSpec((PART, cols), lambda i: (0, i))
    return pl.pallas_call(
        place_body,
        grid=(D // cols,),
        out_shape=jax.ShapeDtypeStruct((ROWS, D), BF),
        in_specs=[pl.BlockSpec(memory_space=pltpu.SMEM)] + [spec] * (HALVES * SECTIONS),
        out_specs=pl.BlockSpec((ROWS, cols), lambda i: (0, i)),
        cost_estimate=cost(2),
        compiler_params=SMALL,
        name="place",
    )(here, *parts)


def exchange(parts):
    return lax.all_to_all(parts, "seq", 0, 0, tiled=True)


def turn(array, by):
    pairs = [(i, (i + by) % SECTIONS) for i in range(SECTIONS)]
    return lax.ppermute(array, "section", pairs)


def local(
    layer_input, query_act, key_act, value_act, output_grad, value_weight, norm_gain, top_grad
):
    weight = lax.all_gather(value_weight[0], "seq", axis=0, tiled=True)
    packed = exchange(pack(query_act[0], output_grad[0], key_act[0], value_act[0]))
    packed = packed.reshape(SEQ, 2 * PACK)
    low, high, inverse, dv = attend_probs(packed)
    dv_parts = exchange(dv.reshape(DEVICES, LOCAL, HEAD_DIM))
    grads = attend_grads(packed, low, high, inverse)
    dv_parts, grads = lax.optimization_barrier((dv_parts, grads))
    here = lax.axis_index("section").astype(jnp.int32).reshape(1)
    terms = norm_term(
        here,
        dv_parts,
        weight,
        layer_input[0].reshape(ROWS, D),
        norm_gain,
        top_grad.reshape(ROWS, D),
    )
    grads_back = exchange(grads.reshape(DEVICES, LOCAL, PACK))
    arrived = [
        [terms[half * SECTIONS]] + [turn(terms[half * SECTIONS + k], k) for k in (1, 2, 3)]
        for half in range(HALVES)
    ]
    back = []
    for half in range(HALVES):
        sums = suffix_sums(here, arrived[half])
        back += [sums[0]] + [turn(sums[k], -k) for k in (1, 2, 3)]
    current = place(here, back)
    query_grad, key_grad = unpack(grads_back)
    return current.reshape(1, BATCH, LOCAL, D), query_grad[None], key_grad[None]


def solution(mesh):
    return jax.shard_map(
        local,
        mesh=mesh,
        in_specs=(
            P("section", None, "seq", None),
            P("section", None, "seq", None),
            P("section", None, "seq", None),
            P("section", None, "seq", None),
            P("section", None, "seq", None),
            P("section", "seq", None),
            P("section", None),
            P(None, "seq", None),
        ),
        out_specs=(
            P("section", None, "seq", None),
            P("section", None, "seq", None),
            P("section", None, "seq", None),
        ),
        check_vma=False,
    )
```
